128 devices in a mesh: band: 4 (over z_lo, core), slab: 32 (over x, y, z_hi).
Axes of the slice: x: 4, y: 4, z: 4 (z_hi: 2, z_lo: 2; z = z_hi * 2 + z_lo), core: 2. Of those that a mesh axis runs over, the one named last changes fastest.
Arguments:
- current_image: float32 [8, 4, 2, 128, 384], P('band', None, None, 'slab'), may hold values from -6 to 6
- langevin_noise: float32 [8, 4, 2, 128, 384], P('band', None, None, 'slab'), may hold values from -6 to 6
- step_size: float32 [1], replicated, may hold values from 0.2 to 0.5
- coil_maps: bfloat16 [8, 4, 32, 2, 128, 384], P(None, None, 'band', None, 'slab'), may hold values from -1 to 1
- measured_kspace: float32 [4, 32, 2, 128, 384], P(None, 'band', None, 'slab'), may hold values from -6 to 6
- sample_mask: int32 [4, 384], replicated, may hold values 0 or 1
- caipi_steps: int32 [8], replicated, may hold values from 0 to 7
- band_order: int32 [8], replicated, may hold values from 0 to 7, each once
- weight_in: bfloat16 [64, 2, 3, 3, 3], replicated, may hold values from -0.875 to 0.875
- weight_mid: bfloat16 [64, 64, 3, 3, 3], replicated, may hold values from -0.15625 to 0.15625
- weight_out: bfloat16 [2, 64, 3, 3, 3], replicated, may hold values from -0.359375 to 0.359375
Outputs:
- next_image: float32 [8, 4, 2, 128, 384], P('band', None, None, 'slab')
The draws below stay inside these ranges and needn't reach their ends.
Inputs may be any that keep to these rules, and one draw needn't show every extreme that they name: `sample_mask`: 1 where a phase-encode line of a slice group was sampled, else 0. `caipi_steps`: shift of a band in units of 48 columns. `band_order`: a permutation of 0 to 7.
All inputs are finite; a program needn't handle non-finite values.
Results may differ from the reference program's by a relative error of at most 0.0039.
Values may be sent and summed in bfloat16 or wider, within the bound.
A program may use at most 128 MiB of HBM per device.

```python
import math
import jax
import jax.numpy as jnp
from jax import lax

NB = 8
NS = 4
Y = 384
C = 32
CH = 64
X = 128


def with_ends(drawn, stream_key, smallest, high):
    extent = drawn.shape
    index_at = [jax.random.randint(jax.random.fold_in(stream_key, axis), (), 0, extent[axis]) for axis in range(len(extent))]
    drawn = drawn.at[tuple(index_at)].set(smallest)
    longest = extent.index(max(extent))
    index_at[longest] = (index_at[longest] + 1) % extent[longest]
    return drawn.at[tuple(index_at)].set(high)


def steps_of(key, shape, cuts, low, largest):
    factor_of, own = 1.0, jax.random.fold_in(key, 6)
    for dim, blocks in cuts:
        steps = jnp.exp(jax.random.uniform(jax.random.fold_in(own, dim), (blocks,), jnp.float32, low / len(cuts), largest / len(cuts)))
        factor_of = factor_of * jnp.repeat(steps, shape[dim] // blocks).reshape([-1 if axis == dim else 1 for axis in range(len(shape))])
    return factor_of


def centred(key, shape, width, bound, cuts=(), dtype=jnp.bfloat16):
    array = jax.random.normal(key, shape, jnp.float32) * width
    if len(cuts) > 0:
        array = steps_of(key, shape, cuts, -0.22, 0.18) * array
    return jnp.clip(array, min=-bound, max=bound).astype(dtype)


def setup_inputs(seed: int = 0) -> dict:
    key_list = jax.random.split(jax.random.key(seed), 12)
    return {
        "current_image": centred(key_list[0], (NB, NS, 2, X, Y), 1.0, 6.0, ((0, 4), (3, 32)), jnp.float32),
        "langevin_noise": centred(key_list[1], (NB, NS, 2, X, Y), 1.0, 6.0, ((0, 4), (3, 32)), jnp.float32),
        "step_size": jnp.clip(jnp.exp(jax.random.uniform(key_list[2], (1,), jnp.float32, math.log(0.2), math.log(0.5))), 0.2, 0.5),
        "coil_maps": centred(key_list[3], (NB, NS, C, 2, X, Y), 0.18, 1.0, ((2, 4), (4, 32))),
        "measured_kspace": centred(key_list[4], (NS, C, 2, X, Y), 1.0, 6.0, ((1, 4), (3, 32)), jnp.float32),
        "sample_mask": with_ends((jax.random.randint(key_list[5], (NS, Y), 0, 3) < 1).astype(jnp.int32), jax.random.fold_in(key_list[5], 1), 0, 1),
        "caipi_steps": with_ends(jax.random.randint(key_list[6], (NB,), 0, 8), jax.random.fold_in(key_list[6], 1), 0, 7).astype(jnp.int32),
        "band_order": jax.random.permutation(key_list[7], NB).astype(jnp.int32),
        "weight_in": centred(key_list[8], (CH, 2, 3, 3, 3), 54 ** -0.5, 0.875),
        "weight_mid": centred(key_list[9], (CH, CH, 3, 3, 3), (CH * 27) ** -0.5, 0.15625),
        "weight_out": centred(key_list[10], (2, CH, 3, 3, 3), 0.06, 0.359375),
    }


def coil_product(coil_field, source):
    real_a = coil_field[..., 0, :, :]
    imag_a = coil_field[..., 1, :, :]
    real_b = source[..., 0, :, :]
    imag_b = source[..., 1, :, :]
    return jnp.stack([real_a * real_b - imag_a * imag_b, real_a * imag_b + imag_a * real_b], axis=-3)

def conjugate_product(coil_field, source):
    real_a = coil_field[..., 0, :, :]
    imag_a = coil_field[..., 1, :, :]
    real_b = source[..., 0, :, :]
    imag_b = source[..., 1, :, :]
    return jnp.stack([real_a * real_b + imag_a * imag_b, real_a * imag_b - imag_a * real_b], axis=-3)

def volume_conv(volume, weight):
    result = lax.conv_general_dilated(volume[None].astype(jnp.float32), weight.astype(jnp.float32), (1, 1, 1), ((1, 1), (1, 1), (1, 1)), dimension_numbers=('NCDHW', 'OIDHW', 'NCDHW'), precision=lax.Precision.HIGHEST)
    return result[0]

def reference(current_image, langevin_noise, step_size, coil_maps, measured_kspace, sample_mask, caipi_steps, band_order, weight_in, weight_mid, weight_out):
    columns = current_image.shape[-1]
    readout = current_image.shape[-2]
    group_slices = current_image.shape[1]
    all_positions = current_image.shape[0]
    caipi_shifts = caipi_steps[band_order] * (columns // 8)
    collapsed = jnp.zeros(measured_kspace.shape, jnp.float32)
    for position in range(all_positions):
        coil_field = coil_maps[position].astype(jnp.float32)
        coil_term = coil_product(coil_field, current_image[position][:, None])
        collapsed = collapsed + jnp.roll(coil_term, caipi_shifts[position], axis=-1)
    signal = lax.complex(collapsed[:, :, 0], collapsed[:, :, 1])
    spectrum = jnp.fft.fft(signal, axis=-1, norm='ortho')
    keep_mask = sample_mask[:, None, None, :].astype(jnp.float32)
    residual_real = keep_mask * (jnp.real(spectrum) - measured_kspace[:, :, 0])
    residual_imag = keep_mask * (jnp.imag(spectrum) - measured_kspace[:, :, 1])
    back_signal = jnp.fft.ifft(lax.complex(residual_real, residual_imag), axis=-1, norm='ortho')
    back_field = jnp.stack([jnp.real(back_signal), jnp.imag(back_signal)], axis=2)
    pieces = []
    for position in range(all_positions):
        coil_field = coil_maps[position].astype(jnp.float32)
        turned = jnp.roll(back_field, -caipi_shifts[position], axis=-1)
        pieces.append(lax.optimization_barrier(jnp.sum(conjugate_product(coil_field, turned), axis=1)))
    consistency = jnp.stack(pieces, axis=0)
    start_field = current_image.astype(jnp.bfloat16)
    volume = jnp.transpose(start_field, (2, 0, 1, 3, 4)).reshape(2, all_positions * group_slices, readout, columns)
    first_features = jax.nn.silu(volume_conv(volume, weight_in)).astype(jnp.bfloat16)
    second_features = jax.nn.silu(volume_conv(first_features, weight_mid)).astype(jnp.bfloat16)
    score_volume = volume_conv(second_features, weight_out)
    score_field = jnp.transpose(score_volume.reshape(2, all_positions, group_slices, readout, columns), (1, 2, 0, 3, 4))
    step_value = step_size[0]
    return current_image + step_value * (score_field - consistency) + jnp.sqrt(2.0 * step_value) * langevin_noise
```

```python
import functools
import math

import jax
import jax.numpy as jnp
import numpy as np
from jax import lax
from jax.experimental import pallas as pl
from jax.experimental.pallas import tpu as pltpu
from jax.sharding import PartitionSpec as P

MESH = pl.DeviceIdType.MESH
F32 = jnp.float32
BF16 = jnp.bfloat16
NB, NS, Y, NC, CH, ROWS = 8, 4, 384, 8, 64, 4
Q = Y // 16
LEAD = (2, 3, 4)


def column_of():
    p = np.arange(Y)
    return (p % 16) * Q + p // 16


def constants():
    col = column_of()
    perm = np.zeros((3, Y, Y), np.float32)
    for dx in range(3):
        for p in range(Y):
            c = col[p] + dx - 1
            if 0 <= c < Y:
                perm[dx, p, c] = 1.0
    k = np.arange(Y)
    phase = (np.outer(k, k) % Y).astype(np.float64) * (2.0 * math.pi / Y)
    table = np.concatenate([np.cos(phase), np.sin(phase)], axis=1) / math.sqrt(Y)
    table = table.astype(np.float32)
    high = table.astype(BF16)
    low = (table - high.astype(np.float32)).astype(BF16)
    row_at = [0, 1, 2, 3, -2, -1, 4, 5]
    place_in = np.zeros((6, 144, 54), np.float32)
    for ro in range(6):
        for dz in range(3):
            for dx in range(3):
                for ch in range(2):
                    for i, row in enumerate(row_at):
                        dy = row - (ro - 1) + 1
                        if 0 <= dy <= 2:
                            t = ((dz * 3 + dy) * 3 + dx) * 2 + ch
                            place_in[ro, dz * 48 + dx * 16 + ch * 8 + i, t] = 0.5
    place_out = np.zeros((4, 144, 54), np.float32)
    for rin in range(4):
        for dz in range(3):
            for dx in range(3):
                for ch in range(2):
                    for ro in range(-1, 5):
                        dy = rin - ro + 1
                        if 0 <= dy <= 2:
                            t = ((dz * 3 + dy) * 3 + dx) * 2 + ch
                            if ro == -1:
                                m = 8 + ch
                            elif ro == 4:
                                m = 10 + ch
                            else:
                                m = ch * 4 + ro
                            place_out[rin, (dz * 3 + dx) * 16 + m, t] = 1.0
    return (
        perm.reshape(3 * Y, Y).astype(BF16),
        high,
        low,
        place_in.astype(BF16),
        place_out.astype(BF16),
    )


def dot_nn(a, b):
    return jnp.dot(a, b, preferred_element_type=F32)


def dot_nt(a, b):
    return lax.dot_general(a, b, (((1,), (1,)), ((), ())), preferred_element_type=F32)


def dot_tn(a, b):
    return lax.dot_general(a, b, (((0,), (0,)), ((), ())), preferred_element_type=F32)


def kernel(
    image, coil, measured, mask_in, steps_in, order_in, w_in, w_mid, w_out,
    perm_in, high_in, low_in, place1_in, place3_in,
    out,
    img, imgbuf, hsend, hrecv, dsend, drecv,
    rsend, rrecv, zsend, zrecv, esend, erecv, csend, crecv,
    coilv, rolled, meas, maskv, steps, order, win, wmid, wout,
    perm, high, low, place1, place3,
    w1, w2, w3, rimg, data, xp, f1, f2, gsum, score, cons,
    local, send_a, recv_a, send_h, recv_h, send_d, recv_d,
    send_r, recv_r, send_z, recv_z, send_e, recv_e, send_c, recv_c,
):
    b = lax.axis_index("band")
    s = lax.axis_index("slab")
    nb = lax.axis_size("band")
    ns = lax.axis_size("slab")

    def at(db, ds_):
        return {"band": lax.rem(b + db + nb, nb), "slab": lax.rem(s + ds_ + ns, ns)}

    partners = [at(k, 0) for k in range(1, nb)] + [at(0, -1), at(0, 1)]
    partners += [at(db, ds_) for db in (-1, 1) for ds_ in (-1, 1)]
    barrier = pltpu.get_barrier_semaphore()
    for who in partners:
        pl.semaphore_signal(barrier, inc=1, device_id=who, device_id_type=MESH)

    groups = {}

    def fetch(name, index, pairs):
        copies = [pltpu.make_async_copy(src, dst, local.at[index, i]) for i, (src, dst) in enumerate(pairs)]
        for c in copies:
            c.start()
        groups[name] = copies

    def arrived(name):
        for c in groups.pop(name):
            c.wait()

    fetch("image", 0, [(image.at[g, t], img.at[g, :, pl.ds(4 * t, 4), :]) for g in range(2) for t in range(4)])
    fetch("scalars", 1, [(steps_in, steps), (order_in, order)])
    for g in range(NB):
        fetch(
            f"coil{g}",
            2 + g,
            [
                (coil.at[g, t, :, r], coilv.at[g, :, r, pl.ds(4 * t, 4), :])
                for t in range(4)
                for r in range(2)
            ],
        )
    fetch("weights", 10, [(w_in, win), (w_mid, wmid), (w_out, wout), (place1_in, place1), (place3_in, place3)])
    fetch("perm", 11, [(perm_in, perm)])
    fetch("tables", 12, [(high_in, high), (low_in, low), (mask_in, maskv)])
    fetch(
        "meas",
        13,
        [(measured.at[t, :, r], meas.at[r, :, pl.ds(4 * t, 4), :]) for t in range(4) for r in range(2)],
    )

    arrived("image")
    own = pl.multiple_of(2 * b, 2)
    for g in range(2):
        for r in range(2):
            imgbuf[own + g, r] = img[g, r].astype(BF16)
    for side in range(2):
        rows = [
            [img[g, r, 4 * t + 2 * side : 4 * t + 2 * side + 2, :] for g in range(2) for t in range(4)]
            for r in range(2)
        ]
        for r in range(2):
            hsend[side, r] = jnp.concatenate(rows[r], axis=0).astype(BF16)
        for zside in range(2):
            z0 = 0 if zside == 0 else 6
            dsend[side, zside] = jnp.concatenate(
                [rows[0][z0], rows[0][z0 + 1], rows[1][z0], rows[1][z0 + 1]], axis=0
            ).astype(BF16)

    def remote(src, dst, ssem, rsem, who):
        return pltpu.make_async_remote_copy(
            src_ref=src, dst_ref=dst, send_sem=ssem, recv_sem=rsem, device_id=who, device_id_type=MESH
        )

    pl.semaphore_wait(barrier, len(partners))
    halo_copies = []
    for side in range(2):
        ds_ = -1 if side == 0 else 1
        halo_copies.append(
            remote(hsend.at[side], hrecv.at[1 - side], send_h.at[side], recv_h.at[1 - side], at(0, ds_))
        )
        for zside in range(2):
            db = -1 if zside == 0 else 1
            i, j = side * 2 + zside, (1 - side) * 2 + (1 - zside)
            halo_copies.append(
                remote(dsend.at[side, zside], drecv.at[1 - side, 1 - zside], send_d.at[i], recv_d.at[j], at(db, ds_))
            )
    image_copies = [
        remote(
            imgbuf.at[pl.ds(own, 2)], imgbuf.at[pl.ds(own, 2)], send_a.at[k - 1], recv_a.at[k - 1], at(k, 0)
        )
        for k in range(1, nb)
    ]
    for c in halo_copies + image_copies:
        c.start()

    arrived("scalars")
    shifts = [steps[order[g]] * (Y // 8) for g in range(NB)]
    for g in range(NB):
        arrived(f"coil{g}")
        for c in range(NC):
            for r in range(2):
                rolled[g, c, r] = pltpu.roll(coilv[g, c, r], shifts[g], 1)

    arrived("weights")
    lane = lax.broadcasted_iota(jnp.int32, (1, 6 * CH), 1)
    inside = ((lane >= CH) | (s > 0)) & ((lane < 5 * CH) | (s < ns - 1))
    w1v = jnp.concatenate([dot_nn(place1[r], win[...]) for r in range(6)], axis=1)
    w1[...] = jnp.where(inside, w1v, 0.0).astype(BF16)
    w3[...] = jnp.concatenate([dot_nn(place3[r], wout[...]) for r in range(4)], axis=1).astype(BF16)
    none = jnp.zeros((CH, CH), F32)
    for dx in range(3):
        for dz in range(3):
            taps = [wmid[(dz * 3 + dy) * 3 + dx].astype(F32) * 0.5 for dy in range(3)]
            for ro in range(2):
                block = taps + [none] if ro == 0 else [none] + taps
                block = jnp.concatenate(block, axis=1).astype(BF16)
                for sl in range(2):
                    k = dx * 4 + dz + sl
                    w2[pl.ds(sl * 128 + ro * CH, CH), pl.ds(k * 256, 256)] = block
        w2[pl.ds(128, 128), pl.ds((dx * 4) * 256, 256)] = jnp.zeros((128, 256), BF16)
        w2[pl.ds(0, 128), pl.ds((dx * 4 + 3) * 256, 256)] = jnp.zeros((128, 256), BF16)

    for c in image_copies:
        c.wait_recv()
    for g in range(NB):
        for r in range(2):
            rimg[g, r] = pltpu.roll(imgbuf[g, r].astype(F32), shifts[g], 1)

    def collapse(c, carry):
        real = jnp.zeros((16, Y), F32)
        imag = jnp.zeros((16, Y), F32)
        for g in range(NB):
            a_re = rolled[g, c, 0].astype(F32)
            a_im = rolled[g, c, 1].astype(F32)
            b_re = rimg[g, 0]
            b_im = rimg[g, 1]
            real += a_re * b_re - a_im * b_im
            imag += a_re * b_im + a_im * b_re
        data[0, c] = real
        data[1, c] = imag
        return carry

    lax.fori_loop(0, NC, collapse, 0)

    for c in halo_copies:
        c.wait_recv()
    arrived("perm")
    low_ok, high_ok = s > 0, s < ns - 1
    tiles = []
    for i in range(12):
        z = i - 2
        pieces = []
        if z < 0:
            slot = lax.max(2 * b - 1, 0)
            t = 4 + z
            ok = b > 0
            halo = [drecv[side, 0] for side in range(2)]
            offset, stride = (z + 2) * 2, 4
        elif z > 7:
            slot = lax.min(2 * b + 2, NB - 1)
            t = z - 8
            ok = b < nb - 1
            halo = [drecv[side, 1] for side in range(2)]
            offset, stride = (z - 8) * 2, 4
        else:
            slot = own + z // 4
            t = z % 4
            ok = None
            halo = None
        for r in range(2):
            mine = imgbuf[slot, r].astype(F32)[4 * t : 4 * t + 4, :]
            if halo is None:
                below = hrecv[0, r].astype(F32)[2 * z : 2 * z + 2, :]
                above = hrecv[1, r].astype(F32)[2 * z : 2 * z + 2, :]
            else:
                o = r * stride + offset
                below = halo[0].astype(F32)[o : o + 2, :]
                above = halo[1].astype(F32)[o : o + 2, :]
            below = jnp.where(low_ok, below, 0.0)
            above = jnp.where(high_ok, above, 0.0)
            pieces += [mine, below, above]
        tile = jnp.concatenate(pieces, axis=0)
        if ok is not None:
            tile = jnp.where(ok, tile, 0.0)
        tiles.append(tile.astype(BF16))
    field = jnp.concatenate(tiles, axis=0)
    for dx in range(3):
        moved = dot_nt(field, perm[pl.ds(dx * Y, Y), :]).astype(BF16)
        for i in range(12):
            xp[pl.ds(i * 48 + dx * 16, 16), :] = moved[16 * i : 16 * i + 16, :]

    sub = lax.broadcasted_iota(jnp.int32, (16, 6 * CH), 0)

    def first(z, carry):
        x = xp[pl.ds(pl.multiple_of(z * 48, 48), 144), :]
        inside_z = ((z > 0) | (b > 0)) & ((z < 9) | (b < nb - 1))
        x = jnp.where(inside_z, x, jnp.zeros_like(x))
        h = dot_tn(x, w1[...])
        f = h + h * jnp.tanh(h)
        f1[z, pl.ds(16, Y), :] = f.astype(BF16)
        left = jnp.where(sub == 0, 0.0, pltpu.roll(f[Y - 16 :, :], 1, 0))
        right = jnp.where(sub == 15, 0.0, pltpu.roll(f[:16, :], 15, 0))
        f1[z, pl.ds(0, 16), :] = left.astype(BF16)
        f1[z, pl.ds(Y + 16, 16), :] = right.astype(BF16)
        return carry

    lax.fori_loop(0, 10, first, 0)

    def middle(zp, carry):
        for rp in range(2):
            lhs = jnp.concatenate(
                [
                    f1[2 * zp + j, pl.ds(16 * dx, Y), pl.ds(rp * 128, 256)]
                    for dx in range(3)
                    for j in range(4)
                ],
                axis=1,
            )
            h = dot_nt(lhs, w2[...])
            f = (h + h * jnp.tanh(h)).astype(BF16)
            f2[2 * zp, :, pl.ds(rp * 128, 128)] = f[:, :128]
            f2[2 * zp + 1, :, pl.ds(rp * 128, 128)] = f[:, 128:]
        return carry

    lax.fori_loop(0, 4, middle, 0)

    gsum[...] = jnp.zeros_like(gsum)

    def last(z, carry):
        part = dot_nt(w3[...], f2[z])
        for dz in range(3):
            for dx in range(3):
                o = (dz * 3 + dx) * 16
                gsum[2 - dx, z + 2 - dz] += part[o : o + 16, :]
        return carry

    lax.fori_loop(0, 8, last, 0)
    total = gsum[...].reshape(3, 160, Y)
    top = total.astype(BF16)
    rest = (total - top.astype(F32)).astype(BF16)
    stacked = jnp.concatenate([jnp.concatenate([top[i], rest[i]], axis=0) for i in range(3)], axis=1)
    both = dot_nn(stacked, perm[...])
    score[...] = (both[:160] + both[160:]).reshape(10, 16, Y)

    for side in range(2):
        o = 8 + 2 * side
        rsend[side] = jnp.concatenate([score[z + 1, o : o + 2, :] for z in range(8)], axis=0).astype(BF16)
        zi = 0 if side == 0 else 9
        zsend[side] = score[zi, 0:8, :].astype(BF16)
        for rside in range(2):
            o = 8 + 2 * rside
            pad = jnp.zeros((6, Y), F32)
            esend[rside, side] = jnp.concatenate([score[zi, o : o + 2, :], pad], axis=0).astype(BF16)
    score_copies = []
    for side in range(2):
        d = -1 if side == 0 else 1
        score_copies.append(
            remote(rsend.at[side], rrecv.at[1 - side], send_r.at[side], recv_r.at[1 - side], at(0, d))
        )
        for zside in range(2):
            db = -1 if zside == 0 else 1
            i, j = side * 2 + zside, (1 - side) * 2 + (1 - zside)
            score_copies.append(
                remote(esend.at[side, zside], erecv.at[1 - side, 1 - zside], send_e.at[i], recv_e.at[j], at(db, d))
            )
    for side in range(2):
        d = -1 if side == 0 else 1
        score_copies.append(
            remote(zsend.at[side], zrecv.at[1 - side], send_z.at[side], recv_z.at[1 - side], at(d, 0))
        )
    for c in score_copies:
        c.start()

    arrived("tables")
    arrived("meas")

    def transform(field):
        flat = field.reshape(2 * NC * 16, Y)
        top = flat.astype(BF16)
        rest = (flat - top.astype(F32)).astype(BF16)
        lhs = jnp.concatenate([top, rest, top], axis=1)
        rhs = jnp.concatenate([high[...], high[...], low[...]], axis=0)
        both = dot_nn(lhs, rhs)
        half = NC * 16
        return both[:half, :Y], both[:half, Y:], both[half:, :Y], both[half:, Y:]

    re_c, re_s, im_c, im_s = transform(data[...])
    keep = maskv[...].astype(F32)
    keep = jnp.concatenate([jnp.broadcast_to(keep[t : t + 1], (4, Y)) for t in range(4)], axis=0)[None]
    data[0] = keep * ((re_c + im_s).reshape(NC, 16, Y) - meas[0])
    data[1] = keep * ((im_c - re_s).reshape(NC, 16, Y) - meas[1])
    re_c, re_s, im_c, im_s = transform(data[...])
    data[0] = (re_c - im_s).reshape(NC, 16, Y)
    data[1] = (im_c + re_s).reshape(NC, 16, Y)

    for g in range(NB):
        real = jnp.zeros((16, Y), F32)
        imag = jnp.zeros((16, Y), F32)
        for c in range(NC):
            a_re = rolled[g, c, 0].astype(F32)
            a_im = rolled[g, c, 1].astype(F32)
            real += a_re * data[0, c] + a_im * data[1, c]
            imag += a_re * data[1, c] - a_im * data[0, c]
        back = lax.rem(Y - shifts[g], Y)
        cons[g, 0] = pltpu.roll(real, back, 1)
        cons[g, 1] = pltpu.roll(imag, back, 1)
        csend[g, 0] = cons[g, 0].astype(BF16)
        csend[g, 1] = cons[g, 1].astype(BF16)
    cons_copies = []
    for k in range(1, nb):
        peer = lax.rem(b + k, nb)
        cons_copies.append(
            remote(
                csend.at[pl.ds(pl.multiple_of(2 * peer, 2), 2)],
                crecv.at[k - 1],
                send_c.at[k - 1],
                recv_c.at[k - 1],
                at(k, 0),
            )
        )
    for c in cons_copies:
        c.start()
    for c in halo_copies + image_copies:
        c.wait_send()

    for c in score_copies:
        c.wait_recv()
    for c in cons_copies:
        c.wait_recv()
    gap = jnp.zeros((2, Y), F32)
    for g in range(2):
        consistency = []
        for r in range(2):
            v = cons[own + g, r]
            for k in range(1, nb):
                v = v + crecv[k - 1, g, r].astype(F32)
            consistency.append(v)
        for t in range(4):
            z = g * 4 + t
            v = score[z + 1, 0:8, :]
            below = jnp.where(low_ok, rrecv[0].astype(F32)[2 * z : 2 * z + 2, :], 0.0)
            above = jnp.where(high_ok, rrecv[1].astype(F32)[2 * z : 2 * z + 2, :], 0.0)
            if z in (0, 7):
                zside = 0 if z == 0 else 1
                ok = b > 0 if z == 0 else b < nb - 1
                v = v + jnp.where(ok, zrecv[zside].astype(F32), 0.0)
                below = below + jnp.where(ok & low_ok, erecv[0, zside].astype(F32)[0:2, :], 0.0)
                above = above + jnp.where(ok & high_ok, erecv[1, zside].astype(F32)[0:2, :], 0.0)
            v = v + jnp.concatenate(
                [below[0:1], gap, above[0:1], below[1:2], gap, above[1:2]], axis=0
            )
            for r in range(2):
                out[g, t, r] = v[4 * r : 4 * r + 4, :] - consistency[r][4 * t : 4 * t + 4, :]
    for c in score_copies + cons_copies:
        c.wait_send()


def per_device(
    current_image,
    langevin_noise,
    step_size,
    coil_maps,
    measured_kspace,
    sample_mask,
    caipi_steps,
    band_order,
    weight_in,
    weight_mid,
    weight_out,
):
    w_in = jnp.transpose(weight_in, (2, 3, 4, 1, 0)).reshape(54, CH)
    w_mid = jnp.transpose(weight_mid, (2, 3, 4, 0, 1)).reshape(27, CH, CH)
    w_out = jnp.transpose(weight_out, (2, 3, 4, 0, 1)).reshape(54, CH)
    consts = [jnp.asarray(c) for c in constants()]
    dma = pltpu.SemaphoreType.DMA
    vmem = pltpu.VMEM
    tile = (16, Y)
    difference = pl.pallas_call(
        kernel,
        out_shape=jax.ShapeDtypeStruct(current_image.shape, F32),
        in_specs=[pl.BlockSpec(memory_space=pl.ANY)] * 14,
        out_specs=pl.BlockSpec(memory_space=pltpu.VMEM),
        scratch_shapes=[
            vmem((2, 2) + tile, F32),
            vmem((NB, 2) + tile, BF16),
            vmem((2, 2) + tile, BF16),
            vmem((2, 2) + tile, BF16),
            vmem((2, 2, 8, Y), BF16),
            vmem((2, 2, 8, Y), BF16),
            vmem((2,) + tile, BF16),
            vmem((2,) + tile, BF16),
            vmem((2, 8, Y), BF16),
            vmem((2, 8, Y), BF16),
            vmem((2, 2, 8, Y), BF16),
            vmem((2, 2, 8, Y), BF16),
            vmem((NB, 2) + tile, BF16),
            vmem((3, 2, 2) + tile, BF16),
            vmem((NB, NC, 2) + tile, BF16),
            vmem((NB, NC, 2) + tile, BF16),
            vmem((2, NC) + tile, F32),
            vmem((NS, Y), jnp.int32),
            pltpu.SMEM((NB,), jnp.int32),
            pltpu.SMEM((NB,), jnp.int32),
            vmem((54, CH), BF16),
            vmem((27, CH, CH), BF16),
            vmem((54, CH), BF16),
            vmem((3 * Y, Y), BF16),
            vmem((Y, 2 * Y), BF16),
            vmem((Y, 2 * Y), BF16),
            vmem((6, 144, 54), BF16),
            vmem((4, 144, 54), BF16),
            vmem((144, 6 * CH), BF16),
            vmem((256, 12 * 256), BF16),
            vmem((144, 4 * CH), BF16),
            vmem((NB, 2) + tile, F32),
            vmem((2, NC) + tile, F32),
            vmem((12 * 48, Y), BF16),
            vmem((10, Y + 32, 6 * CH), BF16),
            vmem((8, Y, 4 * CH), BF16),
            vmem((3, 10) + tile, F32),
            vmem((10,) + tile, F32),
            vmem((NB, 2) + tile, F32),
            dma((14, 8)),
            dma((3,)),
            dma((3,)),
            dma((2,)),
            dma((2,)),
            dma((4,)),
            dma((4,)),
            dma((2,)),
            dma((2,)),
            dma((2,)),
            dma((2,)),
            dma((4,)),
            dma((4,)),
            dma((3,)),
            dma((3,)),
        ],
        compiler_params=pltpu.CompilerParams(collective_id=0, has_side_effects=True),
        name="langevin",
    )(
        current_image, coil_maps, measured_kspace, sample_mask, caipi_steps, band_order,
        w_in, w_mid, w_out, *consts,
    )
    step_value = step_size[0]
    return current_image + step_value * difference + jnp.sqrt(2.0 * step_value) * langevin_noise


def solution(mesh):
    in_specs = (
        P("band", None, None, "slab", None),
        P("band", None, None, "slab", None),
        P(),
        P(None, None, "band", None, "slab", None),
        P(None, "band", None, "slab", None),
        P(),
        P(),
        P(),
        P(),
        P(),
        P(),
    )
    out_specs = P("band", None, None, "slab", None)
    return jax.shard_map(
        per_device, mesh=mesh, in_specs=in_specs, out_specs=out_specs, check_vma=False
    )
```

```python
import functools
import math

import jax
import jax.numpy as jnp
import numpy as np
from jax import lax
from jax.experimental import pallas as pl
from jax.experimental.pallas import tpu as pltpu
from jax.sharding import PartitionSpec as P

MESH = pl.DeviceIdType.MESH
F32 = jnp.float32
BF16 = jnp.bfloat16
NB, NS, Y, NC, CH, ROWS = 8, 4, 384, 8, 64, 4
Q = Y // 16
LEAD = (2, 3, 4)


def column_of():
    p = np.arange(Y)
    return (p % 16) * Q + p // 16


def constants():
    col = column_of()
    perm = np.zeros((3, Y, Y), np.float32)
    for dx in range(3):
        for p in range(Y):
            c = col[p] + dx - 1
            if 0 <= c < Y:
                perm[dx, p, c] = 1.0
    k = np.arange(Y)
    phase = (np.outer(k, k) % Y).astype(np.float64) * (2.0 * math.pi / Y)
    table = np.concatenate([np.cos(phase), np.sin(phase)], axis=1) / math.sqrt(Y)
    table = table.astype(np.float32)
    high = table.astype(BF16)
    low = (table - high.astype(np.float32)).astype(BF16)
    row_at = [0, 1, 2, 3, -2, -1, 4, 5]
    place_in = np.zeros((6, 144, 54), np.float32)
    for ro in range(6):
        for dz in range(3):
            for dx in range(3):
                for ch in range(2):
                    for i, row in enumerate(row_at):
                        dy = row - (ro - 1) + 1
                        if 0 <= dy <= 2:
                            t = ((dz * 3 + dy) * 3 + dx) * 2 + ch
                            place_in[ro, dz * 48 + dx * 16 + ch * 8 + i, t] = 0.5
    place_out = np.zeros((4, 144, 54), np.float32)
    for rin in range(4):
        for dz in range(3):
            for dx in range(3):
                for ch in range(2):
                    for ro in range(-1, 5):
                        dy = rin - ro + 1
                        if 0 <= dy <= 2:
                            t = ((dz * 3 + dy) * 3 + dx) * 2 + ch
                            if ro == -1:
                                m = 8 + ch
                            elif ro == 4:
                                m = 10 + ch
                            else:
                                m = ch * 4 + ro
                            place_out[rin, (dz * 3 + dx) * 16 + m, t] = 1.0
    return (
        perm.reshape(3 * Y, Y).astype(BF16),
        high,
        low,
        place_in.astype(BF16),
        place_out.astype(BF16),
    )


def dot_nn(a, b):
    return jnp.dot(a, b, preferred_element_type=F32)


def dot_nt(a, b):
    return lax.dot_general(a, b, (((1,), (1,)), ((), ())), preferred_element_type=F32)


def dot_tn(a, b):
    return lax.dot_general(a, b, (((0,), (0,)), ((), ())), preferred_element_type=F32)


def kernel(
    image, coil, measured, mask_in, steps_in, order_in, w_in, w_mid, w_out,
    perm_in, high_in, low_in, place1_in, place3_in,
    out,
    img, imgbuf, hsend, hrecv, dsend, drecv, ssend, srecv,
    rsend, rrecv, zsend, zrecv, esend, erecv, csend, crecv,
    coilv, rolled, meas, maskv, steps, order, win, wmid, wout,
    perm, high, low, place1, place3,
    w1, w2, w3, rimg, data, xp, f1, f2, parts, score, cons,
    local, send_a, recv_a, send_h, recv_h, send_d, recv_d, send_s, recv_s,
    send_r, recv_r, send_z, recv_z, send_e, recv_e, send_c, recv_c,
):
    b = lax.axis_index("band")
    s = lax.axis_index("slab")
    nb = lax.axis_size("band")
    ns = lax.axis_size("slab")

    def at(db, ds_):
        return {"band": lax.rem(b + db + nb, nb), "slab": lax.rem(s + ds_ + ns, ns)}

    partners = [at(k, 0) for k in range(1, nb)] + [at(0, -1), at(0, 1)]
    partners += [at(db, ds_) for db in (-1, 1) for ds_ in (-1, 1)]
    barrier = pltpu.get_barrier_semaphore()
    for who in partners:
        pl.semaphore_signal(barrier, inc=1, device_id=who, device_id_type=MESH)

    groups = {}

    def fetch(name, index, pairs):
        copies = [pltpu.make_async_copy(src, dst, local.at[index, i]) for i, (src, dst) in enumerate(pairs)]
        for c in copies:
            c.start()
        groups[name] = copies

    def arrived(name):
        for c in groups.pop(name):
            c.wait()

    fetch("image", 0, [(image.at[g, t], img.at[g, :, pl.ds(4 * t, 4), :]) for g in range(2) for t in range(4)])
    fetch("scalars", 1, [(steps_in, steps), (order_in, order)])
    for g in range(NB):
        fetch(
            f"coil{g}",
            2 + g,
            [
                (coil.at[g, t, :, r], coilv.at[g, :, r, pl.ds(4 * t, 4), :])
                for t in range(4)
                for r in range(2)
            ],
        )
    fetch("weights", 10, [(w_in, win), (w_mid, wmid), (w_out, wout), (place1_in, place1), (place3_in, place3)])
    fetch("perm", 11, [(perm_in, perm)])
    fetch("tables", 12, [(high_in, high), (low_in, low), (mask_in, maskv)])
    fetch(
        "meas",
        13,
        [(measured.at[t, :, r], meas.at[r, :, pl.ds(4 * t, 4), :]) for t in range(4) for r in range(2)],
    )

    arrived("image")
    own = pl.multiple_of(2 * b, 2)
    for g in range(2):
        for r in range(2):
            imgbuf[own + g, r] = img[g, r].astype(BF16)
    for side in range(2):
        rows = [
            [img[g, r, 4 * t + 2 * side : 4 * t + 2 * side + 2, :] for g in range(2) for t in range(4)]
            for r in range(2)
        ]
        for r in range(2):
            hsend[side, r] = jnp.concatenate(rows[r], axis=0).astype(BF16)
        for zside in range(2):
            z0 = 0 if zside == 0 else 6
            dsend[side, zside] = jnp.concatenate(
                [rows[0][z0], rows[0][z0 + 1], rows[1][z0], rows[1][z0 + 1]], axis=0
            ).astype(BF16)
    for r in range(2):
        ssend[0, r] = img[0, r, 0:8, :].astype(BF16)
        ssend[1, r] = img[1, r, 8:16, :].astype(BF16)

    def remote(src, dst, ssem, rsem, who):
        return pltpu.make_async_remote_copy(
            src_ref=src, dst_ref=dst, send_sem=ssem, recv_sem=rsem, device_id=who, device_id_type=MESH
        )

    arrived("weights")
    lane = lax.broadcasted_iota(jnp.int32, (1, 6 * CH), 1)
    inside = ((lane >= CH) | (s > 0)) & ((lane < 5 * CH) | (s < ns - 1))
    flat1 = jnp.concatenate([win[t].astype(F32) for t in range(27)], axis=0).astype(BF16)
    flat3 = jnp.concatenate([wout[t].astype(F32) for t in range(27)], axis=0).astype(BF16)
    w1v = jnp.concatenate([dot_nn(place1[r], flat1) for r in range(6)], axis=1)
    w1[...] = jnp.where(inside, w1v, 0.0).astype(BF16)
    w3[...] = jnp.concatenate([dot_nn(place3[r], flat3) for r in range(4)], axis=1).astype(BF16)
    none = jnp.zeros((CH, CH), F32)
    for dx in range(3):
        for dz in range(3):
            taps = [wmid[(dz * 3 + dy) * 3 + dx].astype(F32) * 0.5 for dy in range(3)]
            for ro in range(2):
                block = taps + [none] if ro == 0 else [none] + taps
                block = jnp.concatenate(block, axis=1).astype(BF16)
                for sl in range(2):
                    k = dx * 4 + dz + sl
                    w2[pl.ds(sl * 128 + ro * CH, CH), pl.ds(k * 256, 256)] = block
        w2[pl.ds(128, 128), pl.ds((dx * 4) * 256, 256)] = jnp.zeros((128, 256), BF16)
        w2[pl.ds(0, 128), pl.ds((dx * 4 + 3) * 256, 256)] = jnp.zeros((128, 256), BF16)

    pl.semaphore_wait(barrier, len(partners))
    halo_copies = []
    for side in range(2):
        ds_ = -1 if side == 0 else 1
        halo_copies.append(
            remote(hsend.at[side], hrecv.at[1 - side], send_h.at[side], recv_h.at[1 - side], at(0, ds_))
        )
        for zside in range(2):
            db = -1 if zside == 0 else 1
            i, j = side * 2 + zside, (1 - side) * 2 + (1 - zside)
            halo_copies.append(
                remote(dsend.at[side, zside], drecv.at[1 - side, 1 - zside], send_d.at[i], recv_d.at[j], at(db, ds_))
            )
    for zside in range(2):
        db = -1 if zside == 0 else 1
        halo_copies.append(
            remote(ssend.at[zside], srecv.at[1 - zside], send_s.at[zside], recv_s.at[1 - zside], at(db, 0))
        )
    image_copies = [
        remote(
            imgbuf.at[pl.ds(own, 2)], imgbuf.at[pl.ds(own, 2)], send_a.at[k - 1], recv_a.at[k - 1], at(k, 0)
        )
        for k in range(1, nb)
    ]
    for c in halo_copies + image_copies:
        c.start()

    arrived("scalars")
    shifts = [steps[order[g]] * (Y // 8) for g in range(NB)]
    for g in range(NB):
        arrived(f"coil{g}")
        for c in range(NC):
            for r in range(2):
                rolled[g, c, r] = pltpu.roll(coilv[g, c, r], shifts[g], 1)

    for c in image_copies:
        c.wait_recv()
    for g in range(NB):
        for r in range(2):
            rimg[g, r] = pltpu.roll(imgbuf[g, r].astype(F32), shifts[g], 1)

    def collapse(c, carry):
        real = jnp.zeros((16, Y), F32)
        imag = jnp.zeros((16, Y), F32)
        for g in range(NB):
            a_re = rolled[g, c, 0].astype(F32)
            a_im = rolled[g, c, 1].astype(F32)
            b_re = rimg[g, 0]
            b_im = rimg[g, 1]
            real += a_re * b_re - a_im * b_im
            imag += a_re * b_im + a_im * b_re
        data[0, c] = real
        data[1, c] = imag
        return carry

    lax.fori_loop(0, NC, collapse, 0)

    arrived("tables")
    arrived("meas")

    def transform(field):
        flat = field.reshape(2 * NC * 16, Y)
        top = flat.astype(BF16)
        rest = (flat - top.astype(F32)).astype(BF16)
        lhs = jnp.concatenate([top, rest, top], axis=1)
        rhs = jnp.concatenate([high[...], high[...], low[...]], axis=0)
        both = dot_nn(lhs, rhs)
        half = NC * 16
        return both[:half, :Y], both[:half, Y:], both[half:, :Y], both[half:, Y:]

    re_c, re_s, im_c, im_s = transform(data[...])
    keep = maskv[...].astype(F32)
    keep = jnp.concatenate([jnp.broadcast_to(keep[t : t + 1], (4, Y)) for t in range(4)], axis=0)[None]
    data[0] = keep * ((re_c + im_s).reshape(NC, 16, Y) - meas[0])
    data[1] = keep * ((im_c - re_s).reshape(NC, 16, Y) - meas[1])
    re_c, re_s, im_c, im_s = transform(data[...])
    data[0] = (re_c - im_s).reshape(NC, 16, Y)
    data[1] = (im_c + re_s).reshape(NC, 16, Y)

    for g in range(NB):
        real = jnp.zeros((16, Y), F32)
        imag = jnp.zeros((16, Y), F32)
        for c in range(NC):
            a_re = rolled[g, c, 0].astype(F32)
            a_im = rolled[g, c, 1].astype(F32)
            real += a_re * data[0, c] + a_im * data[1, c]
            imag += a_re * data[1, c] - a_im * data[0, c]
        back = lax.rem(Y - shifts[g], Y)
        cons[g, 0] = pltpu.roll(real, back, 1)
        cons[g, 1] = pltpu.roll(imag, back, 1)
        csend[g, 0] = cons[g, 0].astype(BF16)
        csend[g, 1] = cons[g, 1].astype(BF16)
    cons_copies = []
    for k in range(1, nb):
        peer = lax.rem(b + k, nb)
        cons_copies.append(
            remote(
                csend.at[pl.ds(pl.multiple_of(2 * peer, 2), 2)],
                crecv.at[k - 1],
                send_c.at[k - 1],
                recv_c.at[k - 1],
                at(k, 0),
            )
        )
    for c in cons_copies:
        c.start()
    for c in halo_copies:
        c.wait_recv()
    arrived("perm")
    low_ok, high_ok = s > 0, s < ns - 1
    tiles = []
    for i in range(12):
        z = i - 2
        pieces = []
        if z < 0:
            t = z + 2
            ok = b > 0
            halo = [drecv[side, 0] for side in range(2)]
            offset, stride = (z + 2) * 2, 4
        elif z > 7:
            t = z - 8
            ok = b < nb - 1
            halo = [drecv[side, 1] for side in range(2)]
            offset, stride = (z - 8) * 2, 4
        else:
            t = z % 4
            ok = None
            halo = None
        for r in range(2):
            if halo is None:
                mine = imgbuf[own + z // 4, r].astype(F32)[4 * t : 4 * t + 4, :]
                below = hrecv[0, r].astype(F32)[2 * z : 2 * z + 2, :]
                above = hrecv[1, r].astype(F32)[2 * z : 2 * z + 2, :]
            else:
                mine = srecv[0 if z < 0 else 1, r].astype(F32)[4 * t : 4 * t + 4, :]
                o = r * stride + offset
                below = halo[0].astype(F32)[o : o + 2, :]
                above = halo[1].astype(F32)[o : o + 2, :]
            below = jnp.where(low_ok, below, 0.0)
            above = jnp.where(high_ok, above, 0.0)
            pieces += [mine, below, above]
        tile = jnp.concatenate(pieces, axis=0)
        if ok is not None:
            tile = jnp.where(ok, tile, 0.0)
        tiles.append(tile.astype(BF16))
    field = jnp.concatenate(tiles, axis=0)
    for dx in range(3):
        moved = dot_nt(field, perm[pl.ds(dx * Y, Y), :]).astype(BF16)
        for i in range(12):
            xp[pl.ds(i * 48 + dx * 16, 16), :] = moved[16 * i : 16 * i + 16, :]

    sub = lax.broadcasted_iota(jnp.int32, (16, 6 * CH), 0)

    for z in range(10):
        x = xp[pl.ds(z * 48, 144), :]
        if z == 0:
            x = jnp.where(b > 0, x, jnp.zeros_like(x))
        if z == 9:
            x = jnp.where(b < nb - 1, x, jnp.zeros_like(x))
        h = dot_tn(x, w1[...])
        f = h + h * jnp.tanh(h)
        f1[z, pl.ds(16, Y), :] = f.astype(BF16)
        left = jnp.where(sub == 0, 0.0, pltpu.roll(f[Y - 16 :, :], 1, 0))
        right = jnp.where(sub == 15, 0.0, pltpu.roll(f[:16, :], 15, 0))
        f1[z, pl.ds(0, 16), :] = left.astype(BF16)
        f1[z, pl.ds(Y + 16, 16), :] = right.astype(BF16)

    def middle(zp, carry):
        for rp in range(2):
            lhs = jnp.concatenate(
                [
                    f1[2 * zp + j, pl.ds(16 * dx, Y), pl.ds(rp * 128, 256)]
                    for dx in range(3)
                    for j in range(4)
                ],
                axis=1,
            )
            h = dot_nt(lhs, w2[...])
            f = (h + h * jnp.tanh(h)).astype(BF16)
            f2[2 * zp, :, pl.ds(rp * 128, 128)] = f[:, :128]
            f2[2 * zp + 1, :, pl.ds(rp * 128, 128)] = f[:, 128:]
        return carry

    lax.fori_loop(0, 4, middle, 0)

    for z in range(8):
        parts[z] = dot_nt(w3[...], f2[z])
    both = []
    for dx in range(3):
        sums = []
        for zo in range(10):
            terms = [
                parts[zo + dz - 2, pl.ds((dz * 3 + dx) * 16, 16), :]
                for dz in range(3)
                if 0 <= zo + dz - 2 < 8
            ]
            sums.append(functools.reduce(jnp.add, terms))
        total = jnp.concatenate(sums, axis=0)
        top = total.astype(BF16)
        rest = (total - top.astype(F32)).astype(BF16)
        both.append(jnp.concatenate([top, rest], axis=0))
    stacked = jnp.concatenate(both[::-1], axis=1)
    both = dot_nn(stacked, perm[...])
    score[...] = (both[:160] + both[160:]).reshape(10, 16, Y)

    for side in range(2):
        o = 8 + 2 * side
        rsend[side] = jnp.concatenate([score[z + 1, o : o + 2, :] for z in range(8)], axis=0).astype(BF16)
        zi = 0 if side == 0 else 9
        zsend[side] = score[zi, 0:8, :].astype(BF16)
        for rside in range(2):
            o = 8 + 2 * rside
            pad = jnp.zeros((6, Y), F32)
            esend[rside, side] = jnp.concatenate([score[zi, o : o + 2, :], pad], axis=0).astype(BF16)
    score_copies = []
    for side in range(2):
        d = -1 if side == 0 else 1
        score_copies.append(
            remote(rsend.at[side], rrecv.at[1 - side], send_r.at[side], recv_r.at[1 - side], at(0, d))
        )
        for zside in range(2):
            db = -1 if zside == 0 else 1
            i, j = side * 2 + zside, (1 - side) * 2 + (1 - zside)
            score_copies.append(
                remote(esend.at[side, zside], erecv.at[1 - side, 1 - zside], send_e.at[i], recv_e.at[j], at(db, d))
            )
    for side in range(2):
        d = -1 if side == 0 else 1
        score_copies.append(
            remote(zsend.at[side], zrecv.at[1 - side], send_z.at[side], recv_z.at[1 - side], at(d, 0))
        )
    for c in score_copies:
        c.start()

    for c in halo_copies + image_copies:
        c.wait_send()

    for c in score_copies:
        c.wait_recv()
    for c in cons_copies:
        c.wait_recv()
    gap = jnp.zeros((2, Y), F32)
    for g in range(2):
        consistency = []
        for r in range(2):
            v = cons[own + g, r]
            for k in range(1, nb):
                v = v + crecv[k - 1, g, r].astype(F32)
            consistency.append(v)
        for t in range(4):
            z = g * 4 + t
            v = score[z + 1, 0:8, :]
            below = jnp.where(low_ok, rrecv[0].astype(F32)[2 * z : 2 * z + 2, :], 0.0)
            above = jnp.where(high_ok, rrecv[1].astype(F32)[2 * z : 2 * z + 2, :], 0.0)
            if z in (0, 7):
                zside = 0 if z == 0 else 1
                ok = b > 0 if z == 0 else b < nb - 1
                v = v + jnp.where(ok, zrecv[zside].astype(F32), 0.0)
                below = below + jnp.where(ok & low_ok, erecv[0, zside].astype(F32)[0:2, :], 0.0)
                above = above + jnp.where(ok & high_ok, erecv[1, zside].astype(F32)[0:2, :], 0.0)
            v = v + jnp.concatenate(
                [below[0:1], gap, above[0:1], below[1:2], gap, above[1:2]], axis=0
            )
            for r in range(2):
                out[g, t, r] = v[4 * r : 4 * r + 4, :] - consistency[r][4 * t : 4 * t + 4, :]
    for c in score_copies + cons_copies:
        c.wait_send()


def per_device(
    current_image,
    langevin_noise,
    step_size,
    coil_maps,
    measured_kspace,
    sample_mask,
    caipi_steps,
    band_order,
    weight_in,
    weight_mid,
    weight_out,
):
    w_in = jnp.transpose(weight_in, (2, 3, 4, 1, 0)).reshape(27, 2, CH)
    w_mid = jnp.transpose(weight_mid, (2, 3, 4, 0, 1)).reshape(27, CH, CH)
    w_out = jnp.transpose(weight_out, (2, 3, 4, 0, 1)).reshape(27, 2, CH)
    consts = [jnp.asarray(c) for c in constants()]
    dma = pltpu.SemaphoreType.DMA
    vmem = pltpu.VMEM
    tile = (16, Y)
    difference = pl.pallas_call(
        kernel,
        out_shape=jax.ShapeDtypeStruct(current_image.shape, F32),
        in_specs=[pl.BlockSpec(memory_space=pl.ANY)] * 14,
        out_specs=pl.BlockSpec(memory_space=pltpu.VMEM),
        scratch_shapes=[
            vmem((2, 2) + tile, F32),
            vmem((NB, 2) + tile, BF16),
            vmem((2, 2) + tile, BF16),
            vmem((2, 2) + tile, BF16),
            vmem((2, 2, 8, Y), BF16),
            vmem((2, 2, 8, Y), BF16),
            vmem((2, 2, 8, Y), BF16),
            vmem((2, 2, 8, Y), BF16),
            vmem((2,) + tile, BF16),
            vmem((2,) + tile, BF16),
            vmem((2, 8, Y), BF16),
            vmem((2, 8, Y), BF16),
            vmem((2, 2, 8, Y), BF16),
            vmem((2, 2, 8, Y), BF16),
            vmem((NB, 2) + tile, BF16),
            vmem((3, 2, 2) + tile, BF16),
            vmem((NB, NC, 2) + tile, BF16),
            vmem((NB, NC, 2) + tile, BF16),
            vmem((2, NC) + tile, F32),
            vmem((NS, Y), jnp.int32),
            pltpu.SMEM((NB,), jnp.int32),
            pltpu.SMEM((NB,), jnp.int32),
            vmem((27, 2, CH), BF16),
            vmem((27, CH, CH), BF16),
            vmem((27, 2, CH), BF16),
            vmem((3 * Y, Y), BF16),
            vmem((Y, 2 * Y), BF16),
            vmem((Y, 2 * Y), BF16),
            vmem((6, 144, 54), BF16),
            vmem((4, 144, 54), BF16),
            vmem((144, 6 * CH), BF16),
            vmem((256, 12 * 256), BF16),
            vmem((144, 4 * CH), BF16),
            vmem((NB, 2) + tile, F32),
            vmem((2, NC) + tile, F32),
            vmem((12 * 48, Y), BF16),
            vmem((10, Y + 32, 6 * CH), BF16),
            vmem((8, Y, 4 * CH), BF16),
            vmem((8, 144, Y), F32),
            vmem((10,) + tile, F32),
            vmem((NB, 2) + tile, F32),
            dma((14, 8)),
            dma((3,)),
            dma((3,)),
            dma((2,)),
            dma((2,)),
            dma((4,)),
            dma((4,)),
            dma((2,)),
            dma((2,)),
            dma((2,)),
            dma((2,)),
            dma((2,)),
            dma((2,)),
            dma((4,)),
            dma((4,)),
            dma((3,)),
            dma((3,)),
        ],
        compiler_params=pltpu.CompilerParams(collective_id=0, has_side_effects=True),
        name="langevin",
    )(
        current_image, coil_maps, measured_kspace, sample_mask, caipi_steps, band_order,
        w_in, w_mid, w_out, *consts,
    )
    step_value = step_size[0]
    return current_image + step_value * difference + jnp.sqrt(2.0 * step_value) * langevin_noise


def solution(mesh):
    in_specs = (
        P("band", None, None, "slab", None),
        P("band", None, None, "slab", None),
        P(),
        P(None, None, "band", None, "slab", None),
        P(None, "band", None, "slab", None),
        P(),
        P(),
        P(),
        P(),
        P(),
        P(),
    )
    out_specs = P("band", None, None, "slab", None)
    return jax.shard_map(
        per_device, mesh=mesh, in_specs=in_specs, out_specs=out_specs, check_vma=False
    )
```

```python
import functools
import math

import jax
import jax.numpy as jnp
import numpy as np
from jax import lax
from jax.experimental import pallas as pl
from jax.experimental.pallas import tpu as pltpu
from jax.sharding import PartitionSpec as P

MESH = pl.DeviceIdType.MESH
F32 = jnp.float32
BF16 = jnp.bfloat16
NB, NS, Y, NC, CH, ROWS = 8, 4, 384, 8, 64, 4
Q = Y // 16
LEAD = (2, 3, 4)


def column_of():
    p = np.arange(Y)
    return (p % 16) * Q + p // 16


def constants():
    col = column_of()
    perm = np.zeros((3, Y, Y), np.float32)
    for dx in range(3):
        for p in range(Y):
            c = col[p] + dx - 1
            if 0 <= c < Y:
                perm[dx, p, c] = 1.0
    k = np.arange(Y)
    phase = (np.outer(k, k) % Y).astype(np.float64) * (2.0 * math.pi / Y)
    table = np.concatenate([np.cos(phase), np.sin(phase)], axis=1) / math.sqrt(Y)
    table = table.astype(np.float32)
    high = table.astype(BF16)
    low = (table - high.astype(np.float32)).astype(BF16)
    row_at = [0, 1, 2, 3, -2, -1, 4, 5]
    place_in = np.zeros((6, 144, 54), np.float32)
    for ro in range(6):
        for dz in range(3):
            for dx in range(3):
                for ch in range(2):
                    for i, row in enumerate(row_at):
                        dy = row - (ro - 1) + 1
                        if 0 <= dy <= 2:
                            t = ((dz * 3 + dy) * 3 + dx) * 2 + ch
                            place_in[ro, dz * 48 + dx * 16 + ch * 8 + i, t] = 0.5
    place_out = np.zeros((4, 144, 54), np.float32)
    for rin in range(4):
        for dz in range(3):
            for dx in range(3):
                for ch in range(2):
                    for ro in range(-1, 5):
                        dy = rin - ro + 1
                        if 0 <= dy <= 2:
                            t = ((dz * 3 + dy) * 3 + dx) * 2 + ch
                            if ro == -1:
                                m = 8 + ch
                            elif ro == 4:
                                m = 10 + ch
                            else:
                                m = ch * 4 + ro
                            place_out[rin, (dz * 3 + dx) * 16 + m, t] = 1.0
    return (
        perm.reshape(3 * Y, Y).astype(BF16),
        high,
        low,
        place_in.astype(BF16),
        place_out.astype(BF16),
    )


def dot_nn(a, b):
    return jnp.dot(a, b, preferred_element_type=F32)


def dot_nt(a, b):
    return lax.dot_general(a, b, (((1,), (1,)), ((), ())), preferred_element_type=F32)


def dot_tn(a, b):
    return lax.dot_general(a, b, (((0,), (0,)), ((), ())), preferred_element_type=F32)


def kernel(
    image, noise_in, step_in, coil, measured, mask_in, steps_in, order_in, w_in, w_mid, w_out,
    perm_in, high_in, low_in, place1_in, place3_in,
    out,
    img, noise, step, imgbuf, hsend, hrecv, dsend, drecv, ssend, srecv,
    rsend, rrecv, zsend, zrecv, esend, erecv, csend, crecv,
    coilv, rolled, meas, maskv, steps, order, win, wmid, wout,
    perm, high, low, place1, place3,
    w1, w2, w3, rimg, data, xp, f1, f2, parts, score, cons,
    local, send_a, recv_a, send_h, recv_h, send_d, recv_d, send_s, recv_s,
    send_r, recv_r, send_z, recv_z, send_e, recv_e, send_c, recv_c,
):
    b = lax.axis_index("band")
    s = lax.axis_index("slab")
    nb = lax.axis_size("band")
    ns = lax.axis_size("slab")

    def at(db, ds_):
        return {"band": lax.rem(b + db + nb, nb), "slab": lax.rem(s + ds_ + ns, ns)}

    partners = [at(k, 0) for k in range(1, nb)] + [at(0, -1), at(0, 1)]
    partners += [at(db, ds_) for db in (-1, 1) for ds_ in (-1, 1)]
    groups = {}

    def fetch(name, index, pairs):
        copies = [pltpu.make_async_copy(src, dst, local.at[index, i]) for i, (src, dst) in enumerate(pairs)]
        for c in copies:
            c.start()
        groups[name] = copies

    def arrived(name):
        for c in groups.pop(name):
            c.wait()

    fetch("image", 0, [(image.at[g, t], img.at[g, :, pl.ds(4 * t, 4), :]) for g in range(2) for t in range(4)])
    barrier = pltpu.get_barrier_semaphore()
    for who in partners:
        pl.semaphore_signal(barrier, inc=1, device_id=who, device_id_type=MESH)

    fetch("scalars", 1, [(steps_in, steps), (order_in, order), (step_in, step)])
    for g in range(NB):
        fetch(
            f"coil{g}",
            2 + g,
            [
                (coil.at[g, t, :, r], coilv.at[g, :, r, pl.ds(4 * t, 4), :])
                for t in range(4)
                for r in range(2)
            ],
        )
    fetch("weights", 10, [(w_in, win), (w_mid, wmid), (w_out, wout), (place1_in, place1), (place3_in, place3)])
    fetch("perm", 11, [(perm_in, perm)])
    fetch("tables", 12, [(high_in, high), (low_in, low), (mask_in, maskv)])
    fetch(
        "meas",
        13,
        [(measured.at[t, :, r], meas.at[r, :, pl.ds(4 * t, 4), :]) for t in range(4) for r in range(2)],
    )
    fetch("noise", 14, [(noise_in.at[g, t], noise.at[g, :, pl.ds(4 * t, 4), :]) for g in range(2) for t in range(4)])

    arrived("image")
    own = pl.multiple_of(2 * b, 2)
    for g in range(2):
        for r in range(2):
            imgbuf[own + g, r] = img[g, r].astype(BF16)
    for side in range(2):
        rows = [
            [img[g, r, 4 * t + 2 * side : 4 * t + 2 * side + 2, :] for g in range(2) for t in range(4)]
            for r in range(2)
        ]
        for r in range(2):
            hsend[side, r] = jnp.concatenate(rows[r], axis=0).astype(BF16)
        for zside in range(2):
            z0 = 0 if zside == 0 else 6
            dsend[side, zside] = jnp.concatenate(
                [rows[0][z0], rows[0][z0 + 1], rows[1][z0], rows[1][z0 + 1]], axis=0
            ).astype(BF16)
    for r in range(2):
        ssend[0, r] = img[0, r, 0:8, :].astype(BF16)
        ssend[1, r] = img[1, r, 8:16, :].astype(BF16)

    def remote(src, dst, ssem, rsem, who):
        return pltpu.make_async_remote_copy(
            src_ref=src, dst_ref=dst, send_sem=ssem, recv_sem=rsem, device_id=who, device_id_type=MESH
        )

    pl.semaphore_wait(barrier, len(partners))
    halo_copies = []
    for side in range(2):
        ds_ = -1 if side == 0 else 1
        halo_copies.append(
            remote(hsend.at[side], hrecv.at[1 - side], send_h.at[side], recv_h.at[1 - side], at(0, ds_))
        )
        for zside in range(2):
            db = -1 if zside == 0 else 1
            i, j = side * 2 + zside, (1 - side) * 2 + (1 - zside)
            halo_copies.append(
                remote(dsend.at[side, zside], drecv.at[1 - side, 1 - zside], send_d.at[i], recv_d.at[j], at(db, ds_))
            )
    for zside in range(2):
        db = -1 if zside == 0 else 1
        halo_copies.append(
            remote(ssend.at[zside], srecv.at[1 - zside], send_s.at[zside], recv_s.at[1 - zside], at(db, 0))
        )
    image_copies = [
        remote(
            imgbuf.at[pl.ds(own, 2)], imgbuf.at[pl.ds(own, 2)], send_a.at[k - 1], recv_a.at[k - 1], at(k, 0)
        )
        for k in range(1, nb)
    ]
    for c in halo_copies + image_copies:
        c.start()

    arrived("weights")
    lane = lax.broadcasted_iota(jnp.int32, (1, 6 * CH), 1)
    inside = ((lane >= CH) | (s > 0)) & ((lane < 5 * CH) | (s < ns - 1))
    flat1 = jnp.concatenate([win[t].astype(F32) for t in range(27)], axis=0).astype(BF16)
    flat3 = jnp.concatenate([wout[t].astype(F32) for t in range(27)], axis=0).astype(BF16)
    w1v = jnp.concatenate([dot_nn(place1[r], flat1) for r in range(6)], axis=1)
    w1[...] = jnp.where(inside, w1v, 0.0).astype(BF16)
    w3[...] = jnp.concatenate([dot_nn(place3[r], flat3) for r in range(4)], axis=1).astype(BF16)
    none = jnp.zeros((CH, CH), F32)
    for dx in range(3):
        for dz in range(3):
            taps = [wmid[(dz * 3 + dy) * 3 + dx].astype(F32) * 0.5 for dy in range(3)]
            for ro in range(2):
                block = taps + [none] if ro == 0 else [none] + taps
                block = jnp.concatenate(block, axis=1).astype(BF16)
                for sl in range(2):
                    k = dx * 4 + dz + sl
                    w2[pl.ds(sl * 128 + ro * CH, CH), pl.ds(k * 256, 256)] = block
        w2[pl.ds(128, 128), pl.ds((dx * 4) * 256, 256)] = jnp.zeros((128, 256), BF16)
        w2[pl.ds(0, 128), pl.ds((dx * 4 + 3) * 256, 256)] = jnp.zeros((128, 256), BF16)

    arrived("scalars")
    shifts = [steps[order[g]] * (Y // 8) for g in range(NB)]
    for g in range(NB):
        arrived(f"coil{g}")
        for c in range(NC):
            for r in range(2):
                rolled[g, c, r] = pltpu.roll(coilv[g, c, r], shifts[g], 1)

    for c in image_copies:
        c.wait_recv()
    for g in range(NB):
        for r in range(2):
            rimg[g, r] = pltpu.roll(imgbuf[g, r].astype(F32), shifts[g], 1)

    def collapse(c, carry):
        real = jnp.zeros((16, Y), F32)
        imag = jnp.zeros((16, Y), F32)
        for g in range(NB):
            a_re = rolled[g, c, 0].astype(F32)
            a_im = rolled[g, c, 1].astype(F32)
            b_re = rimg[g, 0]
            b_im = rimg[g, 1]
            real += a_re * b_re - a_im * b_im
            imag += a_re * b_im + a_im * b_re
        data[0, c] = real
        data[1, c] = imag
        return carry

    lax.fori_loop(0, NC, collapse, 0)

    arrived("tables")
    arrived("meas")

    def transform(field):
        flat = field.reshape(2 * NC * 16, Y)
        top = flat.astype(BF16)
        rest = (flat - top.astype(F32)).astype(BF16)
        lhs = jnp.concatenate([top, rest, top], axis=1)
        rhs = jnp.concatenate([high[...], high[...], low[...]], axis=0)
        both = dot_nn(lhs, rhs)
        half = NC * 16
        return both[:half, :Y], both[:half, Y:], both[half:, :Y], both[half:, Y:]

    re_c, re_s, im_c, im_s = transform(data[...])
    keep = maskv[...].astype(F32)
    keep = jnp.concatenate([jnp.broadcast_to(keep[t : t + 1], (4, Y)) for t in range(4)], axis=0)[None]
    data[0] = keep * ((re_c + im_s).reshape(NC, 16, Y) - meas[0])
    data[1] = keep * ((im_c - re_s).reshape(NC, 16, Y) - meas[1])
    for c in halo_copies:
        c.wait_recv()
    arrived("perm")
    low_ok, high_ok = s > 0, s < ns - 1
    tiles = []
    for i in range(12):
        z = i - 2
        pieces = []
        if z < 0:
            t = z + 2
            ok = b > 0
            halo = [drecv[side, 0] for side in range(2)]
            offset, stride = (z + 2) * 2, 4
        elif z > 7:
            t = z - 8
            ok = b < nb - 1
            halo = [drecv[side, 1] for side in range(2)]
            offset, stride = (z - 8) * 2, 4
        else:
            t = z % 4
            ok = None
            halo = None
        for r in range(2):
            if halo is None:
                mine = imgbuf[own + z // 4, r].astype(F32)[4 * t : 4 * t + 4, :]
                below = hrecv[0, r].astype(F32)[2 * z : 2 * z + 2, :]
                above = hrecv[1, r].astype(F32)[2 * z : 2 * z + 2, :]
            else:
                mine = srecv[0 if z < 0 else 1, r].astype(F32)[4 * t : 4 * t + 4, :]
                o = r * stride + offset
                below = halo[0].astype(F32)[o : o + 2, :]
                above = halo[1].astype(F32)[o : o + 2, :]
            below = jnp.where(low_ok, below, 0.0)
            above = jnp.where(high_ok, above, 0.0)
            pieces += [mine, below, above]
        tile = jnp.concatenate(pieces, axis=0)
        if ok is not None:
            tile = jnp.where(ok, tile, 0.0)
        tiles.append(tile.astype(BF16))
    field = jnp.concatenate(tiles, axis=0)
    for dx in range(3):
        moved = dot_nt(field, perm[pl.ds(dx * Y, Y), :]).astype(BF16)
        for i in range(12):
            xp[pl.ds(i * 48 + dx * 16, 16), :] = moved[16 * i : 16 * i + 16, :]

    sub = lax.broadcasted_iota(jnp.int32, (16, 6 * CH), 0)

    for z in range(10):
        x = xp[pl.ds(z * 48, 144), :]
        if z == 0:
            x = jnp.where(b > 0, x, jnp.zeros_like(x))
        if z == 9:
            x = jnp.where(b < nb - 1, x, jnp.zeros_like(x))
        h = dot_tn(x, w1[...])
        f = h + h * jnp.tanh(h)
        f1[z, pl.ds(16, Y), :] = f.astype(BF16)
        left = jnp.where(sub == 0, 0.0, pltpu.roll(f[Y - 16 :, :], 1, 0))
        right = jnp.where(sub == 15, 0.0, pltpu.roll(f[:16, :], 15, 0))
        f1[z, pl.ds(0, 16), :] = left.astype(BF16)
        f1[z, pl.ds(Y + 16, 16), :] = right.astype(BF16)

    def middle(zp, carry):
        for rp in range(2):
            lhs = jnp.concatenate(
                [
                    f1[2 * zp + j, pl.ds(16 * dx, Y), pl.ds(rp * 128, 256)]
                    for dx in range(3)
                    for j in range(4)
                ],
                axis=1,
            )
            h = dot_nt(lhs, w2[...])
            f = (h + h * jnp.tanh(h)).astype(BF16)
            f2[2 * zp, :, pl.ds(rp * 128, 128)] = f[:, :128]
            f2[2 * zp + 1, :, pl.ds(rp * 128, 128)] = f[:, 128:]
        return carry

    lax.fori_loop(0, 4, middle, 0)

    for z in range(8):
        parts[z] = dot_nt(w3[...], f2[z])
    both = []
    for dx in range(3):
        sums = []
        for zo in range(10):
            terms = [
                parts[zo + dz - 2, pl.ds((dz * 3 + dx) * 16, 16), :]
                for dz in range(3)
                if 0 <= zo + dz - 2 < 8
            ]
            sums.append(functools.reduce(jnp.add, terms))
        total = jnp.concatenate(sums, axis=0)
        top = total.astype(BF16)
        rest = (total - top.astype(F32)).astype(BF16)
        both.append(jnp.concatenate([top, rest], axis=0))
    stacked = jnp.concatenate(both[::-1], axis=1)
    both = dot_nn(stacked, perm[...])
    score[...] = (both[:160] + both[160:]).reshape(10, 16, Y)

    for side in range(2):
        o = 8 + 2 * side
        rsend[side] = jnp.concatenate([score[z + 1, o : o + 2, :] for z in range(8)], axis=0).astype(BF16)
        zi = 0 if side == 0 else 9
        zsend[side] = score[zi, 0:8, :].astype(BF16)
        for rside in range(2):
            o = 8 + 2 * rside
            pad = jnp.zeros((6, Y), F32)
            esend[rside, side] = jnp.concatenate([score[zi, o : o + 2, :], pad], axis=0).astype(BF16)
    score_copies = []
    for side in range(2):
        d = -1 if side == 0 else 1
        score_copies.append(
            remote(rsend.at[side], rrecv.at[1 - side], send_r.at[side], recv_r.at[1 - side], at(0, d))
        )
        for zside in range(2):
            db = -1 if zside == 0 else 1
            i, j = side * 2 + zside, (1 - side) * 2 + (1 - zside)
            score_copies.append(
                remote(esend.at[side, zside], erecv.at[1 - side, 1 - zside], send_e.at[i], recv_e.at[j], at(db, d))
            )
    for side in range(2):
        d = -1 if side == 0 else 1
        score_copies.append(
            remote(zsend.at[side], zrecv.at[1 - side], send_z.at[side], recv_z.at[1 - side], at(d, 0))
        )
    for c in score_copies:
        c.start()

    re_c, re_s, im_c, im_s = transform(data[...])
    data[0] = (re_c - im_s).reshape(NC, 16, Y)
    data[1] = (im_c + re_s).reshape(NC, 16, Y)

    cons_copies = []
    for k in (1, 2, 3, 0):
        peer = lax.rem(b + k, nb)
        for i in range(2):
            g = 2 * peer + i
            real = jnp.zeros((16, Y), F32)
            imag = jnp.zeros((16, Y), F32)
            for c in range(NC):
                a_re = rolled[g, c, 0].astype(F32)
                a_im = rolled[g, c, 1].astype(F32)
                real += a_re * data[0, c] + a_im * data[1, c]
                imag += a_re * data[1, c] - a_im * data[0, c]
            back = lax.rem(Y - steps[order[g]] * (Y // 8), Y)
            real = pltpu.roll(real, back, 1)
            imag = pltpu.roll(imag, back, 1)
            if k > 0:
                csend[k - 1, i, 0] = real.astype(BF16)
                csend[k - 1, i, 1] = imag.astype(BF16)
            else:
                cons[i, 0] = real
                cons[i, 1] = imag
        if k > 0:
            copy = remote(csend.at[k - 1], crecv.at[k - 1], send_c.at[k - 1], recv_c.at[k - 1], at(k, 0))
            copy.start()
            cons_copies.append(copy)

    for c in halo_copies + image_copies:
        c.wait_send()

    arrived("noise")
    size = jnp.full((16, Y), step[0], F32)
    spread = jnp.sqrt(2.0 * size)
    for g in range(2):
        for r in range(2):
            cons[g, r] = img[g, r] + spread * noise[g, r] - size * cons[g, r]
    for c in score_copies:
        c.wait_recv()
    for c in cons_copies:
        c.wait_recv()
    gap = jnp.zeros((2, Y), F32)
    for g in range(2):
        consistency = []
        for r in range(2):
            v = cons[g, r]
            for k in range(1, nb):
                v = v - size * crecv[k - 1, g, r].astype(F32)
            consistency.append(v)
        for t in range(4):
            z = g * 4 + t
            v = score[z + 1, 0:8, :]
            below = jnp.where(low_ok, rrecv[0].astype(F32)[2 * z : 2 * z + 2, :], 0.0)
            above = jnp.where(high_ok, rrecv[1].astype(F32)[2 * z : 2 * z + 2, :], 0.0)
            if z in (0, 7):
                zside = 0 if z == 0 else 1
                ok = b > 0 if z == 0 else b < nb - 1
                v = v + jnp.where(ok, zrecv[zside].astype(F32), 0.0)
                below = below + jnp.where(ok & low_ok, erecv[0, zside].astype(F32)[0:2, :], 0.0)
                above = above + jnp.where(ok & high_ok, erecv[1, zside].astype(F32)[0:2, :], 0.0)
            v = v + jnp.concatenate(
                [below[0:1], gap, above[0:1], below[1:2], gap, above[1:2]], axis=0
            )
            for r in range(2):
                out[g, t, r] = size[0:4] * v[4 * r : 4 * r + 4, :] + consistency[r][4 * t : 4 * t + 4, :]
    for c in score_copies + cons_copies:
        c.wait_send()


def per_device(
    current_image,
    langevin_noise,
    step_size,
    coil_maps,
    measured_kspace,
    sample_mask,
    caipi_steps,
    band_order,
    weight_in,
    weight_mid,
    weight_out,
):
    w_in = jnp.transpose(weight_in, (2, 3, 4, 1, 0)).reshape(27, 2, CH)
    w_mid = jnp.transpose(weight_mid, (2, 3, 4, 0, 1)).reshape(27, CH, CH)
    w_out = jnp.transpose(weight_out, (2, 3, 4, 0, 1)).reshape(27, 2, CH)
    consts = [jnp.asarray(c) for c in constants()]
    dma = pltpu.SemaphoreType.DMA
    vmem = pltpu.VMEM
    tile = (16, Y)
    return pl.pallas_call(
        kernel,
        out_shape=jax.ShapeDtypeStruct(current_image.shape, F32),
        in_specs=[pl.BlockSpec(memory_space=pl.ANY)] * 16,
        out_specs=pl.BlockSpec(memory_space=pltpu.VMEM),
        scratch_shapes=[
            vmem((2, 2) + tile, F32),
            vmem((2, 2) + tile, F32),
            pltpu.SMEM((1,), F32),
            vmem((NB, 2) + tile, BF16),
            vmem((2, 2) + tile, BF16),
            vmem((2, 2) + tile, BF16),
            vmem((2, 2, 8, Y), BF16),
            vmem((2, 2, 8, Y), BF16),
            vmem((2, 2, 8, Y), BF16),
            vmem((2, 2, 8, Y), BF16),
            vmem((2,) + tile, BF16),
            vmem((2,) + tile, BF16),
            vmem((2, 8, Y), BF16),
            vmem((2, 8, Y), BF16),
            vmem((2, 2, 8, Y), BF16),
            vmem((2, 2, 8, Y), BF16),
            vmem((3, 2, 2) + tile, BF16),
            vmem((3, 2, 2) + tile, BF16),
            vmem((NB, NC, 2) + tile, BF16),
            vmem((NB, NC, 2) + tile, BF16),
            vmem((2, NC) + tile, F32),
            vmem((NS, Y), jnp.int32),
            pltpu.SMEM((NB,), jnp.int32),
            pltpu.SMEM((NB,), jnp.int32),
            vmem((27, 2, CH), BF16),
            vmem((27, CH, CH), BF16),
            vmem((27, 2, CH), BF16),
            vmem((3 * Y, Y), BF16),
            vmem((Y, 2 * Y), BF16),
            vmem((Y, 2 * Y), BF16),
            vmem((6, 144, 54), BF16),
            vmem((4, 144, 54), BF16),
            vmem((144, 6 * CH), BF16),
            vmem((256, 12 * 256), BF16),
            vmem((144, 4 * CH), BF16),
            vmem((NB, 2) + tile, F32),
            vmem((2, NC) + tile, F32),
            vmem((12 * 48, Y), BF16),
            vmem((10, Y + 32, 6 * CH), BF16),
            vmem((8, Y, 4 * CH), BF16),
            vmem((8, 144, Y), F32),
            vmem((10,) + tile, F32),
            vmem((2, 2) + tile, F32),
            dma((15, 8)),
            dma((3,)),
            dma((3,)),
            dma((2,)),
            dma((2,)),
            dma((4,)),
            dma((4,)),
            dma((2,)),
            dma((2,)),
            dma((2,)),
            dma((2,)),
            dma((2,)),
            dma((2,)),
            dma((4,)),
            dma((4,)),
            dma((3,)),
            dma((3,)),
        ],
        compiler_params=pltpu.CompilerParams(collective_id=0, has_side_effects=True),
        name="langevin",
    )(
        current_image, langevin_noise, step_size, coil_maps, measured_kspace, sample_mask, caipi_steps, band_order,
        w_in, w_mid, w_out, *consts,
    )


def solution(mesh):
    in_specs = (
        P("band", None, None, "slab", None),
        P("band", None, None, "slab", None),
        P(),
        P(None, None, "band", None, "slab", None),
        P(None, "band", None, "slab", None),
        P(),
        P(),
        P(),
        P(),
        P(),
        P(),
    )
    out_specs = P("band", None, None, "slab", None)
    return jax.shard_map(
        per_device, mesh=mesh, in_specs=in_specs, out_specs=out_specs, check_vma=False
    )
```

```python
import functools
import math

import jax
import jax.numpy as jnp
import numpy as np
from jax import lax
from jax.experimental import pallas as pl
from jax.experimental.pallas import tpu as pltpu
from jax.sharding import PartitionSpec as P

MESH = pl.DeviceIdType.MESH
F32 = jnp.float32
BF16 = jnp.bfloat16
NB, NS, Y, NC, CH, ROWS = 8, 4, 384, 8, 64, 4
Q = Y // 16
LEAD = (2, 3, 4)


def column_of():
    p = np.arange(Y)
    return (p % 16) * Q + p // 16


def constants():
    col = column_of()
    perm = np.zeros((3, Y, Y), np.float32)
    for dx in range(3):
        for p in range(Y):
            c = col[p] + dx - 1
            if 0 <= c < Y:
                perm[dx, p, c] = 1.0
    k = np.arange(Y)
    phase = (np.outer(k, k) % Y).astype(np.float64) * (2.0 * math.pi / Y)
    table = np.concatenate([np.cos(phase), np.sin(phase)], axis=1) / math.sqrt(Y)
    table = table.astype(np.float32)
    high = table.astype(BF16)
    low = (table - high.astype(np.float32)).astype(BF16)
    row_at = [0, 1, 2, 3, -2, -1, 4, 5]
    place_in = np.zeros((6, 144, 54), np.float32)
    for ro in range(6):
        for dz in range(3):
            for dx in range(3):
                for ch in range(2):
                    for i, row in enumerate(row_at):
                        dy = row - (ro - 1) + 1
                        if 0 <= dy <= 2:
                            t = ((dz * 3 + dy) * 3 + dx) * 2 + ch
                            place_in[ro, dz * 48 + dx * 16 + ch * 8 + i, t] = 0.5
    place_out = np.zeros((4, 144, 54), np.float32)
    for rin in range(4):
        for dz in range(3):
            for dx in range(3):
                for ch in range(2):
                    for ro in range(-1, 5):
                        dy = rin - ro + 1
                        if 0 <= dy <= 2:
                            t = ((dz * 3 + dy) * 3 + dx) * 2 + ch
                            if ro == -1:
                                m = 8 + ch
                            elif ro == 4:
                                m = 10 + ch
                            else:
                                m = ch * 4 + ro
                            place_out[rin, (dz * 3 + dx) * 16 + m, t] = 1.0
    return (
        perm.reshape(3 * Y, Y).astype(BF16),
        high,
        low,
        place_in.astype(BF16),
        place_out.astype(BF16),
    )


def dot_nn(a, b):
    return jnp.dot(a, b, preferred_element_type=F32)


def dot_nt(a, b):
    return lax.dot_general(a, b, (((1,), (1,)), ((), ())), preferred_element_type=F32)


def dot_tn(a, b):
    return lax.dot_general(a, b, (((0,), (0,)), ((), ())), preferred_element_type=F32)


def kernel(
    image, noise_in, step_in, coil, measured, mask_in, steps_in, order_in, w_in, w_mid, w_out,
    perm_in, high_in, low_in, place1_in, place3_in,
    out,
    img, noise, step, imgbuf, hsend, hrecv, dsend, drecv, ssend, srecv,
    rsend, rrecv, zsend, zrecv, esend, erecv, csend, crecv,
    coilv, rolled, meas, maskv, steps, order, win, wmid, wout,
    perm, high, low, place1, place3,
    w1, w2, w3, rimg, data, xp, f1, f2, parts, score, cons,
    local, send_a, recv_a, send_h, recv_h, send_d, recv_d, send_s, recv_s,
    send_r, recv_r, send_z, recv_z, send_e, recv_e, send_c, recv_c,
):
    b = lax.axis_index("band")
    s = lax.axis_index("slab")
    nb = lax.axis_size("band")
    ns = lax.axis_size("slab")

    def at(db, ds_):
        return {"band": lax.rem(b + db + nb, nb), "slab": lax.rem(s + ds_ + ns, ns)}

    low_ok, high_ok = s > 0, s < ns - 1
    other = 1 - 2 * lax.rem(b, 2)
    across = lax.rem(b + 2, nb)
    peers = [across + other, across, b + other]
    groups = {}

    def fetch(name, index, pairs):
        copies = [pltpu.make_async_copy(src, dst, local.at[index, i]) for i, (src, dst) in enumerate(pairs)]
        for c in copies:
            c.start()
        groups[name] = copies

    def arrived(name):
        for c in groups.pop(name):
            c.wait()

    fetch("image", 0, [(image.at[g, t], img.at[g, :, pl.ds(4 * t, 4), :]) for g in range(2) for t in range(4)])
    barrier = pltpu.get_barrier_semaphore()

    def greet(ds_):
        for db in (0, -1, 1):
            pl.semaphore_signal(barrier, inc=1, device_id=at(db, ds_), device_id_type=MESH)

    pl.when(low_ok)(lambda: greet(-1))
    pl.when(high_ok)(lambda: greet(1))
    for peer in peers:
        pl.semaphore_signal(barrier, inc=1, device_id={"band": peer, "slab": s}, device_id_type=MESH)

    fetch("scalars", 1, [(steps_in, steps), (order_in, order), (step_in, step)])
    fetch("weights", 10, [(w_in, win), (w_mid, wmid), (w_out, wout), (place1_in, place1), (place3_in, place3)])
    fetch("perm", 11, [(perm_in, perm)])
    arrived("image")
    own = pl.multiple_of(2 * b, 2)
    for g in range(2):
        for r in range(2):
            imgbuf[own + g, r] = img[g, r].astype(BF16)
    for side in range(2):
        rows = [
            [img[g, r, 4 * t + 2 * side : 4 * t + 2 * side + 2, :] for g in range(2) for t in range(4)]
            for r in range(2)
        ]
        for r in range(2):
            hsend[side, r] = jnp.concatenate(rows[r], axis=0).astype(BF16)
        for zside in range(2):
            z0 = 0 if zside == 0 else 6
            dsend[side, zside] = jnp.concatenate(
                [rows[0][z0], rows[0][z0 + 1], rows[1][z0], rows[1][z0 + 1]], axis=0
            ).astype(BF16)
    for r in range(2):
        ssend[0, r] = img[0, r, 0:8, :].astype(BF16)
        ssend[1, r] = img[1, r, 8:16, :].astype(BF16)

    def remote(src, dst, ssem, rsem, who):
        return pltpu.make_async_remote_copy(
            src_ref=src, dst_ref=dst, send_sem=ssem, recv_sem=rsem, device_id=who, device_id_type=MESH
        )

    sides = (s + ns - 1) // ns + (2 * ns - 2 - s) // ns
    pl.semaphore_wait(barrier, len(peers) + 3 * sides)
    halo_copies = [[], [], []]
    for side in range(2):
        ds_ = -1 if side == 0 else 1
        halo_copies[side].append(
            remote(hsend.at[side], hrecv.at[1 - side], send_h.at[side], recv_h.at[1 - side], at(0, ds_))
        )
        for zside in range(2):
            db = -1 if zside == 0 else 1
            i, j = side * 2 + zside, (1 - side) * 2 + (1 - zside)
            halo_copies[side].append(
                remote(dsend.at[side, zside], drecv.at[1 - side, 1 - zside], send_d.at[i], recv_d.at[j], at(db, ds_))
            )
    for zside in range(2):
        db = -1 if zside == 0 else 1
        halo_copies[2].append(
            remote(ssend.at[zside], srecv.at[1 - zside], send_s.at[zside], recv_s.at[1 - zside], at(db, 0))
        )
    image_copies = [
        remote(
            imgbuf.at[pl.ds(own, 2)], imgbuf.at[pl.ds(own, 2)], send_a.at[k], recv_a.at[k],
            {"band": peer, "slab": s},
        )
        for k, peer in enumerate(peers)
    ]

    def every(copies, verb):
        for c in copies:
            getattr(c, verb)()

    def sent_by_side(copies, verb):
        pl.when(low_ok)(lambda: every(copies[0], verb))
        pl.when(high_ok)(lambda: every(copies[1], verb))
        every(copies[2], verb)

    def wait_arrivals(copies):
        pl.when(high_ok)(lambda: every(copies[0], "wait_recv"))
        pl.when(low_ok)(lambda: every(copies[1], "wait_recv"))
        every(copies[2], "wait_recv")

    sent_by_side(halo_copies, "start")
    every(image_copies, "start")

    for g in range(NB):
        fetch(
            f"coil{g}",
            2 + g,
            [
                (coil.at[g, t, :, r], coilv.at[g, :, r, pl.ds(4 * t, 4), :])
                for t in range(4)
                for r in range(2)
            ],
        )
    fetch("tables", 12, [(high_in, high), (low_in, low), (mask_in, maskv)])
    fetch(
        "meas",
        13,
        [(measured.at[t, :, r], meas.at[r, :, pl.ds(4 * t, 4), :]) for t in range(4) for r in range(2)],
    )
    fetch("noise", 14, [(noise_in.at[g, t], noise.at[g, :, pl.ds(4 * t, 4), :]) for g in range(2) for t in range(4)])

    arrived("weights")
    lane = lax.broadcasted_iota(jnp.int32, (1, 6 * CH), 1)
    inside = ((lane >= CH) | (s > 0)) & ((lane < 5 * CH) | (s < ns - 1))
    flat1 = jnp.concatenate([win[t].astype(F32) for t in range(27)], axis=0).astype(BF16)
    flat3 = jnp.concatenate([wout[t].astype(F32) for t in range(27)], axis=0).astype(BF16)
    w1v = jnp.concatenate([dot_nn(place1[r], flat1) for r in range(6)], axis=1)
    w1[...] = jnp.where(inside, w1v, 0.0).astype(BF16)
    w3[...] = jnp.concatenate([dot_nn(place3[r], flat3) for r in range(4)], axis=1).astype(BF16)
    none = jnp.zeros((CH, CH), F32)
    for dx in range(3):
        for dz in range(3):
            taps = [wmid[(dz * 3 + dy) * 3 + dx].astype(F32) * 0.5 for dy in range(3)]
            for ro in range(2):
                block = taps + [none] if ro == 0 else [none] + taps
                block = jnp.concatenate(block, axis=1).astype(BF16)
                for sl in range(2):
                    k = dx * 4 + dz + sl
                    w2[pl.ds(sl * 128 + ro * CH, CH), pl.ds(k * 256, 256)] = block
        w2[pl.ds(128, 128), pl.ds((dx * 4) * 256, 256)] = jnp.zeros((128, 256), BF16)
        w2[pl.ds(0, 128), pl.ds((dx * 4 + 3) * 256, 256)] = jnp.zeros((128, 256), BF16)

    arrived("scalars")
    shifts = [steps[order[g]] * (Y // 8) for g in range(NB)]
    for g in range(NB):
        arrived(f"coil{g}")
        for c in range(NC):
            for r in range(2):
                rolled[g, c, r] = pltpu.roll(coilv[g, c, r], shifts[g], 1)

    wait_arrivals(halo_copies)
    arrived("perm")
    tiles = []
    for i in range(12):
        z = i - 2
        pieces = []
        if z < 0:
            t = z + 2
            ok = b > 0
            halo = [drecv[side, 0] for side in range(2)]
            offset, stride = (z + 2) * 2, 4
        elif z > 7:
            t = z - 8
            ok = b < nb - 1
            halo = [drecv[side, 1] for side in range(2)]
            offset, stride = (z - 8) * 2, 4
        else:
            t = z % 4
            ok = None
            halo = None
        for r in range(2):
            if halo is None:
                mine = imgbuf[own + z // 4, r].astype(F32)[4 * t : 4 * t + 4, :]
                below = hrecv[0, r].astype(F32)[2 * z : 2 * z + 2, :]
                above = hrecv[1, r].astype(F32)[2 * z : 2 * z + 2, :]
            else:
                mine = srecv[0 if z < 0 else 1, r].astype(F32)[4 * t : 4 * t + 4, :]
                o = r * stride + offset
                below = halo[0].astype(F32)[o : o + 2, :]
                above = halo[1].astype(F32)[o : o + 2, :]
            below = jnp.where(low_ok, below, 0.0)
            above = jnp.where(high_ok, above, 0.0)
            pieces += [mine, below, above]
        tile = jnp.concatenate(pieces, axis=0)
        if ok is not None:
            tile = jnp.where(ok, tile, 0.0)
        tiles.append(tile.astype(BF16))
    field = jnp.concatenate(tiles, axis=0)
    for dx in range(3):
        moved = dot_nt(field, perm[pl.ds(dx * Y, Y), :]).astype(BF16)
        for i in range(12):
            xp[pl.ds(i * 48 + dx * 16, 16), :] = moved[16 * i : 16 * i + 16, :]

    sub = lax.broadcasted_iota(jnp.int32, (16, 6 * CH), 0)

    for z in range(10):
        x = xp[pl.ds(z * 48, 144), :]
        if z == 0:
            x = jnp.where(b > 0, x, jnp.zeros_like(x))
        if z == 9:
            x = jnp.where(b < nb - 1, x, jnp.zeros_like(x))
        h = dot_tn(x, w1[...])
        f = h + h * jnp.tanh(h)
        f1[z, pl.ds(16, Y), :] = f.astype(BF16)
        left = jnp.where(sub == 0, 0.0, pltpu.roll(f[Y - 16 :, :], 1, 0))
        right = jnp.where(sub == 15, 0.0, pltpu.roll(f[:16, :], 15, 0))
        f1[z, pl.ds(0, 16), :] = left.astype(BF16)
        f1[z, pl.ds(Y + 16, 16), :] = right.astype(BF16)

    every(image_copies, "wait_recv")
    for g in range(NB):
        for r in range(2):
            rimg[g, r] = pltpu.roll(imgbuf[g, r].astype(F32), shifts[g], 1)

    def collapse(c):
        real = jnp.zeros((16, Y), F32)
        imag = jnp.zeros((16, Y), F32)
        for g in range(NB):
            a_re = rolled[g, c, 0].astype(F32)
            a_im = rolled[g, c, 1].astype(F32)
            b_re = rimg[g, 0]
            b_im = rimg[g, 1]
            real += a_re * b_re - a_im * b_im
            imag += a_re * b_im + a_im * b_re
        data[0, c] = real
        data[1, c] = imag

    def middle(zp, carry):
        for i in range(2):
            collapse(2 * zp + i)
        for rp in range(2):
            lhs = jnp.concatenate(
                [
                    f1[2 * zp + j, pl.ds(16 * dx, Y), pl.ds(rp * 128, 256)]
                    for dx in range(3)
                    for j in range(4)
                ],
                axis=1,
            )
            h = dot_nt(lhs, w2[...])
            f = (h + h * jnp.tanh(h)).astype(BF16)
            f2[2 * zp, :, pl.ds(rp * 128, 128)] = f[:, :128]
            f2[2 * zp + 1, :, pl.ds(rp * 128, 128)] = f[:, 128:]
        return carry

    lax.fori_loop(0, 4, middle, 0)

    for z in range(8):
        parts[z] = dot_nt(w3[...], f2[z])
    both = []
    for dx in range(3):
        sums = []
        for zo in range(10):
            terms = [
                parts[zo + dz - 2, pl.ds((dz * 3 + dx) * 16, 16), :]
                for dz in range(3)
                if 0 <= zo + dz - 2 < 8
            ]
            sums.append(functools.reduce(jnp.add, terms))
        total = jnp.concatenate(sums, axis=0)
        top = total.astype(BF16)
        rest = (total - top.astype(F32)).astype(BF16)
        both.append(jnp.concatenate([top, rest], axis=0))
    stacked = jnp.concatenate(both[::-1], axis=1)
    both = dot_nn(stacked, perm[...])
    score[...] = (both[:160] + both[160:]).reshape(10, 16, Y)

    for side in range(2):
        o = 8 + 2 * side
        rsend[side] = jnp.concatenate([score[z + 1, o : o + 2, :] for z in range(8)], axis=0).astype(BF16)
        zi = 0 if side == 0 else 9
        zsend[side] = score[zi, 0:8, :].astype(BF16)
        for rside in range(2):
            o = 8 + 2 * rside
            pad = jnp.zeros((6, Y), F32)
            esend[rside, side] = jnp.concatenate([score[zi, o : o + 2, :], pad], axis=0).astype(BF16)
    score_copies = [[], [], []]
    for side in range(2):
        d = -1 if side == 0 else 1
        score_copies[side].append(
            remote(rsend.at[side], rrecv.at[1 - side], send_r.at[side], recv_r.at[1 - side], at(0, d))
        )
        for zside in range(2):
            db = -1 if zside == 0 else 1
            i, j = side * 2 + zside, (1 - side) * 2 + (1 - zside)
            score_copies[side].append(
                remote(esend.at[side, zside], erecv.at[1 - side, 1 - zside], send_e.at[i], recv_e.at[j], at(db, d))
            )
    for side in range(2):
        d = -1 if side == 0 else 1
        score_copies[2].append(
            remote(zsend.at[side], zrecv.at[1 - side], send_z.at[side], recv_z.at[1 - side], at(d, 0))
        )
    sent_by_side(score_copies, "start")

    arrived("tables")
    arrived("meas")

    def transform(field):
        flat = field.reshape(2 * NC * 16, Y)
        top = flat.astype(BF16)
        rest = (flat - top.astype(F32)).astype(BF16)
        lhs = jnp.concatenate([top, rest, top], axis=1)
        rhs = jnp.concatenate([high[...], high[...], low[...]], axis=0)
        both = dot_nn(lhs, rhs)
        half = NC * 16
        return both[:half, :Y], both[:half, Y:], both[half:, :Y], both[half:, Y:]

    re_c, re_s, im_c, im_s = transform(data[...])
    keep = maskv[...].astype(F32)
    keep = jnp.concatenate([jnp.broadcast_to(keep[t : t + 1], (4, Y)) for t in range(4)], axis=0)[None]
    data[0] = keep * ((re_c + im_s).reshape(NC, 16, Y) - meas[0])
    data[1] = keep * ((im_c - re_s).reshape(NC, 16, Y) - meas[1])
    re_c, re_s, im_c, im_s = transform(data[...])
    data[0] = (re_c - im_s).reshape(NC, 16, Y)
    data[1] = (im_c + re_s).reshape(NC, 16, Y)

    cons_copies = []
    for k, peer in enumerate(peers + [b]):
        for i in range(2):
            g = 2 * peer + i
            real = jnp.zeros((16, Y), F32)
            imag = jnp.zeros((16, Y), F32)
            for c in range(NC):
                a_re = rolled[g, c, 0].astype(F32)
                a_im = rolled[g, c, 1].astype(F32)
                real += a_re * data[0, c] + a_im * data[1, c]
                imag += a_re * data[1, c] - a_im * data[0, c]
            back = lax.rem(Y - steps[order[g]] * (Y // 8), Y)
            real = pltpu.roll(real, back, 1)
            imag = pltpu.roll(imag, back, 1)
            if k < 3:
                csend[k, i, 0] = real.astype(BF16)
                csend[k, i, 1] = imag.astype(BF16)
            else:
                cons[i, 0] = real
                cons[i, 1] = imag
        if k < 3:
            who = {"band": peer, "slab": s}
            copy = remote(csend.at[k], crecv.at[k], send_c.at[k], recv_c.at[k], who)
            copy.start()
            cons_copies.append(copy)

    sent_by_side(halo_copies, "wait_send")
    every(image_copies, "wait_send")

    arrived("noise")
    size = jnp.full((16, Y), step[0], F32)
    spread = jnp.sqrt(2.0 * size)
    for g in range(2):
        for r in range(2):
            cons[g, r] = img[g, r] + spread * noise[g, r] - size * cons[g, r]
    wait_arrivals(score_copies)
    every(cons_copies, "wait_recv")
    gap = jnp.zeros((2, Y), F32)
    for g in range(2):
        consistency = []
        for r in range(2):
            v = cons[g, r]
            for k in range(1, nb):
                v = v - size * crecv[k - 1, g, r].astype(F32)
            consistency.append(v)
        for t in range(4):
            z = g * 4 + t
            v = score[z + 1, 0:8, :]
            below = jnp.where(low_ok, rrecv[0].astype(F32)[2 * z : 2 * z + 2, :], 0.0)
            above = jnp.where(high_ok, rrecv[1].astype(F32)[2 * z : 2 * z + 2, :], 0.0)
            if z in (0, 7):
                zside = 0 if z == 0 else 1
                ok = b > 0 if z == 0 else b < nb - 1
                v = v + jnp.where(ok, zrecv[zside].astype(F32), 0.0)
                below = below + jnp.where(ok & low_ok, erecv[0, zside].astype(F32)[0:2, :], 0.0)
                above = above + jnp.where(ok & high_ok, erecv[1, zside].astype(F32)[0:2, :], 0.0)
            v = v + jnp.concatenate(
                [below[0:1], gap, above[0:1], below[1:2], gap, above[1:2]], axis=0
            )
            for r in range(2):
                out[g, t, r] = size[0:4] * v[4 * r : 4 * r + 4, :] + consistency[r][4 * t : 4 * t + 4, :]
    sent_by_side(score_copies, "wait_send")
    every(cons_copies, "wait_send")


def per_device(
    current_image,
    langevin_noise,
    step_size,
    coil_maps,
    measured_kspace,
    sample_mask,
    caipi_steps,
    band_order,
    weight_in,
    weight_mid,
    weight_out,
):
    w_in = jnp.transpose(weight_in, (2, 3, 4, 1, 0)).reshape(27, 2, CH)
    w_mid = jnp.transpose(weight_mid, (2, 3, 4, 0, 1)).reshape(27, CH, CH)
    w_out = jnp.transpose(weight_out, (2, 3, 4, 0, 1)).reshape(27, 2, CH)
    consts = [jnp.asarray(c) for c in constants()]
    dma = pltpu.SemaphoreType.DMA
    vmem = pltpu.VMEM
    tile = (16, Y)
    return pl.pallas_call(
        kernel,
        out_shape=jax.ShapeDtypeStruct(current_image.shape, F32),
        in_specs=[pl.BlockSpec(memory_space=pl.ANY)] * 16,
        out_specs=pl.BlockSpec(memory_space=pltpu.VMEM),
        scratch_shapes=[
            vmem((2, 2) + tile, F32),
            vmem((2, 2) + tile, F32),
            pltpu.SMEM((1,), F32),
            vmem((NB, 2) + tile, BF16),
            vmem((2, 2) + tile, BF16),
            vmem((2, 2) + tile, BF16),
            vmem((2, 2, 8, Y), BF16),
            vmem((2, 2, 8, Y), BF16),
            vmem((2, 2, 8, Y), BF16),
            vmem((2, 2, 8, Y), BF16),
            vmem((2,) + tile, BF16),
            vmem((2,) + tile, BF16),
            vmem((2, 8, Y), BF16),
            vmem((2, 8, Y), BF16),
            vmem((2, 2, 8, Y), BF16),
            vmem((2, 2, 8, Y), BF16),
            vmem((3, 2, 2) + tile, BF16),
            vmem((3, 2, 2) + tile, BF16),
            vmem((NB, NC, 2) + tile, BF16),
            vmem((NB, NC, 2) + tile, BF16),
            vmem((2, NC) + tile, F32),
            vmem((NS, Y), jnp.int32),
            pltpu.SMEM((NB,), jnp.int32),
            pltpu.SMEM((NB,), jnp.int32),
            vmem((27, 2, CH), BF16),
            vmem((27, CH, CH), BF16),
            vmem((27, 2, CH), BF16),
            vmem((3 * Y, Y), BF16),
            vmem((Y, 2 * Y), BF16),
            vmem((Y, 2 * Y), BF16),
            vmem((6, 144, 54), BF16),
            vmem((4, 144, 54), BF16),
            vmem((144, 6 * CH), BF16),
            vmem((256, 12 * 256), BF16),
            vmem((144, 4 * CH), BF16),
            vmem((NB, 2) + tile, F32),
            vmem((2, NC) + tile, F32),
            vmem((12 * 48, Y), BF16),
            vmem((10, Y + 32, 6 * CH), BF16),
            vmem((8, Y, 4 * CH), BF16),
            vmem((8, 144, Y), F32),
            vmem((10,) + tile, F32),
            vmem((2, 2) + tile, F32),
            dma((15, 8)),
            dma((3,)),
            dma((3,)),
            dma((2,)),
            dma((2,)),
            dma((4,)),
            dma((4,)),
            dma((2,)),
            dma((2,)),
            dma((2,)),
            dma((2,)),
            dma((2,)),
            dma((2,)),
            dma((4,)),
            dma((4,)),
            dma((3,)),
            dma((3,)),
        ],
        compiler_params=pltpu.CompilerParams(collective_id=0, has_side_effects=True),
        name="langevin",
    )(
        current_image, langevin_noise, step_size, coil_maps, measured_kspace, sample_mask, caipi_steps, band_order,
        w_in, w_mid, w_out, *consts,
    )


def solution(mesh):
    in_specs = (
        P("band", None, None, "slab", None),
        P("band", None, None, "slab", None),
        P(),
        P(None, None, "band", None, "slab", None),
        P(None, "band", None, "slab", None),
        P(),
        P(),
        P(),
        P(),
        P(),
        P(),
    )
    out_specs = P("band", None, None, "slab", None)
    return jax.shard_map(
        per_device, mesh=mesh, in_specs=in_specs, out_specs=out_specs, check_vma=False
    )
```

```python
import functools
import math

import jax
import jax.numpy as jnp
import numpy as np
from jax import lax
from jax.experimental import pallas as pl
from jax.experimental.pallas import tpu as pltpu
from jax.sharding import PartitionSpec as P

MESH = pl.DeviceIdType.MESH
F32 = jnp.float32
BF16 = jnp.bfloat16
NB, NS, Y, NC, CH, ROWS = 8, 4, 384, 8, 64, 4
Q = Y // 16
LEAD = (2, 3, 4)


def column_of():
    p = np.arange(Y)
    return (p % 16) * Q + p // 16


def constants():
    col = column_of()
    perm = np.zeros((3, Y, Y), np.float32)
    for dx in range(3):
        for p in range(Y):
            c = col[p] + dx - 1
            if 0 <= c < Y:
                perm[dx, p, c] = 1.0
    k = np.arange(Y)
    phase = (np.outer(k, k) % Y).astype(np.float64) * (2.0 * math.pi / Y)
    table = np.concatenate([np.cos(phase), np.sin(phase)], axis=1) / math.sqrt(Y)
    table = table.astype(np.float32)
    high = table.astype(BF16)
    low = (table - high.astype(np.float32)).astype(BF16)
    row_at = [0, 1, 2, 3, -2, -1, 4, 5]
    place_in = np.zeros((6, 144, 54), np.float32)
    for ro in range(6):
        for dz in range(3):
            for dx in range(3):
                for ch in range(2):
                    for i, row in enumerate(row_at):
                        dy = row - (ro - 1) + 1
                        if 0 <= dy <= 2:
                            t = ((dz * 3 + dy) * 3 + dx) * 2 + ch
                            place_in[ro, dz * 48 + dx * 16 + ch * 8 + i, t] = 0.5
    place_out = np.zeros((4, 144, 54), np.float32)
    for rin in range(4):
        for dz in range(3):
            for dx in range(3):
                for ch in range(2):
                    for ro in range(-1, 5):
                        dy = rin - ro + 1
                        if 0 <= dy <= 2:
                            t = ((dz * 3 + dy) * 3 + dx) * 2 + ch
                            if ro == -1:
                                m = 8 + ch
                            elif ro == 4:
                                m = 10 + ch
                            else:
                                m = ch * 4 + ro
                            place_out[rin, (dz * 3 + dx) * 16 + m, t] = 1.0
    return (
        perm.reshape(3 * Y, Y).astype(BF16),
        high,
        low,
        place_in.astype(BF16),
        place_out.astype(BF16),
    )


def dot_nn(a, b):
    return jnp.dot(a, b, preferred_element_type=F32)


def dot_nt(a, b):
    return lax.dot_general(a, b, (((1,), (1,)), ((), ())), preferred_element_type=F32)


def dot_tn(a, b):
    return lax.dot_general(a, b, (((0,), (0,)), ((), ())), preferred_element_type=F32)


def kernel(
    image, noise_in, step_in, coil, measured, mask_in, steps_in, order_in, w_in, w_mid, w_out,
    perm_in, high_in, low_in, place1_in, place3_in,
    out,
    img, noise, step, imgbuf, hsend, hrecv, dsend, drecv, ssend, srecv,
    rsend, rrecv, zsend, zrecv, esend, erecv, csend, crecv,
    coilv, rolled, meas, maskv, steps, order, win, wmid, wout,
    perm, high, low, place1, place3,
    w1, w2, w2e, w3, rimg, data, xp, f1, f2, parts, score, cons,
    local, send_a, recv_a, send_h, recv_h, send_d, recv_d, send_s, recv_s,
    send_r, recv_r, send_z, recv_z, send_e, recv_e, send_c, recv_c,
):
    b = lax.axis_index("band")
    s = lax.axis_index("slab")
    nb = lax.axis_size("band")
    ns = lax.axis_size("slab")

    def at(db, ds_):
        return {"band": lax.rem(b + db + nb, nb), "slab": lax.rem(s + ds_ + ns, ns)}

    low_ok, high_ok = s > 0, s < ns - 1
    other = 1 - 2 * lax.rem(b, 2)
    across = lax.rem(b + 2, nb)
    peers = [across + other, across, b + other]
    groups = {}

    def fetch(name, index, pairs):
        copies = [pltpu.make_async_copy(src, dst, local.at[index, i]) for i, (src, dst) in enumerate(pairs)]
        for c in copies:
            c.start()
        groups[name] = copies

    def arrived(name):
        for c in groups.pop(name):
            c.wait()

    fetch("image", 0, [(image.at[g, t], img.at[g, :, pl.ds(4 * t, 4), :]) for g in range(2) for t in range(4)])
    barrier = pltpu.get_barrier_semaphore()

    def greet(ds_):
        for db in (0, -1, 1):
            pl.semaphore_signal(barrier, inc=1, device_id=at(db, ds_), device_id_type=MESH)

    pl.when(low_ok)(lambda: greet(-1))
    pl.when(high_ok)(lambda: greet(1))
    for peer in peers:
        pl.semaphore_signal(barrier, inc=1, device_id={"band": peer, "slab": s}, device_id_type=MESH)

    fetch("scalars", 1, [(steps_in, steps), (order_in, order), (step_in, step)])
    fetch("weights", 10, [(w_in, win), (w_mid, wmid), (w_out, wout), (place1_in, place1), (place3_in, place3)])
    fetch("perm", 11, [(perm_in, perm)])
    arrived("image")
    own = pl.multiple_of(2 * b, 2)
    for g in range(2):
        for r in range(2):
            imgbuf[own + g, r] = img[g, r].astype(BF16)
    for side in range(2):
        rows = [
            [img[g, r, 4 * t + 2 * side : 4 * t + 2 * side + 2, :] for g in range(2) for t in range(4)]
            for r in range(2)
        ]
        for r in range(2):
            hsend[side, r] = jnp.concatenate(rows[r], axis=0).astype(BF16)
        for zside in range(2):
            z0 = 0 if zside == 0 else 6
            dsend[side, zside] = jnp.concatenate(
                [rows[0][z0], rows[0][z0 + 1], rows[1][z0], rows[1][z0 + 1]], axis=0
            ).astype(BF16)
    for r in range(2):
        ssend[0, r] = img[0, r, 0:8, :].astype(BF16)
        ssend[1, r] = img[1, r, 8:16, :].astype(BF16)

    def remote(src, dst, ssem, rsem, who):
        return pltpu.make_async_remote_copy(
            src_ref=src, dst_ref=dst, send_sem=ssem, recv_sem=rsem, device_id=who, device_id_type=MESH
        )

    sides = (s + ns - 1) // ns + (2 * ns - 2 - s) // ns
    pl.semaphore_wait(barrier, len(peers) + 3 * sides)
    halo_copies = [[], [], []]
    for side in range(2):
        ds_ = -1 if side == 0 else 1
        halo_copies[side].append(
            remote(hsend.at[side], hrecv.at[1 - side], send_h.at[side], recv_h.at[1 - side], at(0, ds_))
        )
        for zside in range(2):
            db = -1 if zside == 0 else 1
            i, j = side * 2 + zside, (1 - side) * 2 + (1 - zside)
            halo_copies[side].append(
                remote(dsend.at[side, zside], drecv.at[1 - side, 1 - zside], send_d.at[i], recv_d.at[j], at(db, ds_))
            )
    for zside in range(2):
        db = -1 if zside == 0 else 1
        halo_copies[2].append(
            remote(ssend.at[zside], srecv.at[1 - zside], send_s.at[zside], recv_s.at[1 - zside], at(db, 0))
        )
    image_copies = [
        remote(
            imgbuf.at[pl.ds(own, 2)], imgbuf.at[pl.ds(own, 2)], send_a.at[k], recv_a.at[k],
            {"band": peer, "slab": s},
        )
        for k, peer in enumerate(peers)
    ]

    def every(copies, verb):
        for c in copies:
            getattr(c, verb)()

    def sent_by_side(copies, verb):
        pl.when(low_ok)(lambda: every(copies[0], verb))
        pl.when(high_ok)(lambda: every(copies[1], verb))
        every(copies[2], verb)

    def wait_arrivals(copies):
        pl.when(high_ok)(lambda: every(copies[0], "wait_recv"))
        pl.when(low_ok)(lambda: every(copies[1], "wait_recv"))
        every(copies[2], "wait_recv")

    sent_by_side(halo_copies, "start")
    every(image_copies, "start")

    for g in range(NB):
        fetch(
            f"coil{g}",
            2 + g,
            [
                (coil.at[g, t, :, r], coilv.at[g, :, r, pl.ds(4 * t, 4), :])
                for t in range(4)
                for r in range(2)
            ],
        )
    fetch("tables", 12, [(high_in, high), (low_in, low), (mask_in, maskv)])
    fetch(
        "meas",
        13,
        [(measured.at[t, :, r], meas.at[r, :, pl.ds(4 * t, 4), :]) for t in range(4) for r in range(2)],
    )
    fetch("noise", 14, [(noise_in.at[g, t], noise.at[g, :, pl.ds(4 * t, 4), :]) for g in range(2) for t in range(4)])

    arrived("weights")
    lane = lax.broadcasted_iota(jnp.int32, (1, 6 * CH), 1)
    inside = ((lane >= CH) | (s > 0)) & ((lane < 5 * CH) | (s < ns - 1))
    flat1 = jnp.concatenate([win[t].astype(F32) for t in range(27)], axis=0).astype(BF16)
    flat3 = jnp.concatenate([wout[t].astype(F32) for t in range(27)], axis=0).astype(BF16)
    w1v = jnp.concatenate([dot_nn(place1[r], flat1) for r in range(6)], axis=1)
    w1[...] = jnp.where(inside, w1v, 0.0).astype(BF16)
    w3[...] = jnp.concatenate([dot_nn(place3[r], flat3) for r in range(4)], axis=1).astype(BF16)
    none = jnp.zeros((CH, CH), F32)
    for dx in range(3):
        for dz in range(3):
            taps = [wmid[(dz * 3 + dy) * 3 + dx].astype(F32) * 0.5 for dy in range(3)]
            for ro in range(2):
                block = taps + [none] if ro == 0 else [none] + taps
                block = jnp.concatenate(block, axis=1).astype(BF16)
                for sl in range(2):
                    j = dz + sl
                    if j in (1, 2):
                        w2[pl.ds(sl * 128 + ro * CH, CH), pl.ds((dx * 2 + j - 1) * 256, 256)] = block
                    elif dx == 1:
                        w2[pl.ds(sl * 128 + ro * CH, CH), pl.ds((6 + sl) * 256, 256)] = block
                    else:
                        w2e[sl, pl.ds(dx // 2 * 128 + ro * CH, CH), :] = block
    w2[pl.ds(128, 128), pl.ds(6 * 256, 256)] = jnp.zeros((128, 256), BF16)
    w2[pl.ds(0, 128), pl.ds(7 * 256, 256)] = jnp.zeros((128, 256), BF16)

    arrived("scalars")
    shifts = [steps[order[g]] * (Y // 8) for g in range(NB)]
    for g in range(NB):
        arrived(f"coil{g}")
        for c in range(NC):
            for r in range(2):
                rolled[g, c, r] = pltpu.roll(coilv[g, c, r], shifts[g], 1)

    wait_arrivals(halo_copies)
    arrived("perm")
    tiles = []
    for i in range(12):
        z = i - 2
        pieces = []
        if z < 0:
            t = z + 2
            ok = b > 0
            halo = [drecv[side, 0] for side in range(2)]
            offset, stride = (z + 2) * 2, 4
        elif z > 7:
            t = z - 8
            ok = b < nb - 1
            halo = [drecv[side, 1] for side in range(2)]
            offset, stride = (z - 8) * 2, 4
        else:
            t = z % 4
            ok = None
            halo = None
        for r in range(2):
            if halo is None:
                mine = imgbuf[own + z // 4, r].astype(F32)[4 * t : 4 * t + 4, :]
                below = hrecv[0, r].astype(F32)[2 * z : 2 * z + 2, :]
                above = hrecv[1, r].astype(F32)[2 * z : 2 * z + 2, :]
            else:
                mine = srecv[0 if z < 0 else 1, r].astype(F32)[4 * t : 4 * t + 4, :]
                o = r * stride + offset
                below = halo[0].astype(F32)[o : o + 2, :]
                above = halo[1].astype(F32)[o : o + 2, :]
            below = jnp.where(low_ok, below, 0.0)
            above = jnp.where(high_ok, above, 0.0)
            pieces += [mine, below, above]
        tile = jnp.concatenate(pieces, axis=0)
        if ok is not None:
            tile = jnp.where(ok, tile, 0.0)
        tiles.append(tile.astype(BF16))
    field = jnp.concatenate(tiles, axis=0)
    for dx in range(3):
        moved = dot_nt(field, perm[pl.ds(dx * Y, Y), :]).astype(BF16)
        for i in range(12):
            xp[pl.ds(i * 48 + dx * 16, 16), :] = moved[16 * i : 16 * i + 16, :]

    sub = lax.broadcasted_iota(jnp.int32, (16, 6 * CH), 0)

    for z in range(10):
        x = xp[pl.ds(z * 48, 144), :]
        if z == 0:
            x = jnp.where(b > 0, x, jnp.zeros_like(x))
        if z == 9:
            x = jnp.where(b < nb - 1, x, jnp.zeros_like(x))
        h = dot_tn(x, w1[...])
        f = h + h * jnp.tanh(h)
        f1[z, pl.ds(16, Y), :] = f.astype(BF16)
        left = jnp.where(sub == 0, 0.0, pltpu.roll(f[Y - 16 :, :], 1, 0))
        right = jnp.where(sub == 15, 0.0, pltpu.roll(f[:16, :], 15, 0))
        f1[z, pl.ds(0, 16), :] = left.astype(BF16)
        f1[z, pl.ds(Y + 16, 16), :] = right.astype(BF16)

    every(image_copies, "wait_recv")
    for g in range(NB):
        for r in range(2):
            rimg[g, r] = pltpu.roll(imgbuf[g, r].astype(F32), shifts[g], 1)

    def collapse(c):
        real = jnp.zeros((16, Y), F32)
        imag = jnp.zeros((16, Y), F32)
        for g in range(NB):
            a_re = rolled[g, c, 0].astype(F32)
            a_im = rolled[g, c, 1].astype(F32)
            b_re = rimg[g, 0]
            b_im = rimg[g, 1]
            real += a_re * b_re - a_im * b_im
            imag += a_re * b_im + a_im * b_re
        data[0, c] = real
        data[1, c] = imag

    def middle(zp, carry):
        for i in range(2):
            collapse(2 * zp + i)
        for rp in range(2):
            lanes = pl.ds(rp * 128, 256)
            views = [f1[2 * zp + j, pl.ds(16 * dx, Y), lanes] for dx in range(3) for j in (1, 2)]
            views += [f1[2 * zp + j, pl.ds(16, Y), lanes] for j in (0, 3)]
            h = dot_nt(jnp.concatenate(views, axis=1), w2[...])
            for sl in range(2):
                side = dot_nt(f1[2 * zp + 3 * sl, :, lanes], w2e[sl])
                v = h[:, sl * 128 : sl * 128 + 128] + side[:Y, :128] + side[32:, 128:]
                f2[2 * zp + sl, :, pl.ds(rp * 128, 128)] = (v + v * jnp.tanh(v)).astype(BF16)
        return carry

    lax.fori_loop(0, 4, middle, 0)

    for z in range(8):
        parts[z] = dot_nt(w3[...], f2[z])
    both = []
    for dx in range(3):
        sums = []
        for zo in range(10):
            terms = [
                parts[zo + dz - 2, pl.ds((dz * 3 + dx) * 16, 16), :]
                for dz in range(3)
                if 0 <= zo + dz - 2 < 8
            ]
            sums.append(functools.reduce(jnp.add, terms))
        total = jnp.concatenate(sums, axis=0)
        top = total.astype(BF16)
        rest = (total - top.astype(F32)).astype(BF16)
        both.append(jnp.concatenate([top, rest], axis=0))
    stacked = jnp.concatenate(both[::-1], axis=1)
    both = dot_nn(stacked, perm[...])
    score[...] = (both[:160] + both[160:]).reshape(10, 16, Y)

    for side in range(2):
        o = 8 + 2 * side
        rsend[side] = jnp.concatenate([score[z + 1, o : o + 2, :] for z in range(8)], axis=0).astype(BF16)
        zi = 0 if side == 0 else 9
        zsend[side] = score[zi, 0:8, :].astype(BF16)
        for rside in range(2):
            o = 8 + 2 * rside
            pad = jnp.zeros((6, Y), F32)
            esend[rside, side] = jnp.concatenate([score[zi, o : o + 2, :], pad], axis=0).astype(BF16)
    score_copies = [[], [], []]
    for side in range(2):
        d = -1 if side == 0 else 1
        score_copies[side].append(
            remote(rsend.at[side], rrecv.at[1 - side], send_r.at[side], recv_r.at[1 - side], at(0, d))
        )
        for zside in range(2):
            db = -1 if zside == 0 else 1
            i, j = side * 2 + zside, (1 - side) * 2 + (1 - zside)
            score_copies[side].append(
                remote(esend.at[side, zside], erecv.at[1 - side, 1 - zside], send_e.at[i], recv_e.at[j], at(db, d))
            )
    for side in range(2):
        d = -1 if side == 0 else 1
        score_copies[2].append(
            remote(zsend.at[side], zrecv.at[1 - side], send_z.at[side], recv_z.at[1 - side], at(d, 0))
        )
    sent_by_side(score_copies, "start")

    arrived("tables")
    arrived("meas")

    def transform(field):
        flat = field.reshape(2 * NC * 16, Y)
        top = flat.astype(BF16)
        rest = (flat - top.astype(F32)).astype(BF16)
        lhs = jnp.concatenate([top, rest, top], axis=1)
        rhs = jnp.concatenate([high[...], high[...], low[...]], axis=0)
        both = dot_nn(lhs, rhs)
        half = NC * 16
        return both[:half, :Y], both[:half, Y:], both[half:, :Y], both[half:, Y:]

    re_c, re_s, im_c, im_s = transform(data[...])
    keep = maskv[...].astype(F32)
    keep = jnp.concatenate([jnp.broadcast_to(keep[t : t + 1], (4, Y)) for t in range(4)], axis=0)[None]
    data[0] = keep * ((re_c + im_s).reshape(NC, 16, Y) - meas[0])
    data[1] = keep * ((im_c - re_s).reshape(NC, 16, Y) - meas[1])
    re_c, re_s, im_c, im_s = transform(data[...])
    data[0] = (re_c - im_s).reshape(NC, 16, Y)
    data[1] = (im_c + re_s).reshape(NC, 16, Y)

    cons_copies = []
    for k, peer in enumerate(peers + [b]):
        for i in range(2):
            g = 2 * peer + i
            real = jnp.zeros((16, Y), F32)
            imag = jnp.zeros((16, Y), F32)
            for c in range(NC):
                a_re = rolled[g, c, 0].astype(F32)
                a_im = rolled[g, c, 1].astype(F32)
                real += a_re * data[0, c] + a_im * data[1, c]
                imag += a_re * data[1, c] - a_im * data[0, c]
            back = lax.rem(Y - steps[order[g]] * (Y // 8), Y)
            real = pltpu.roll(real, back, 1)
            imag = pltpu.roll(imag, back, 1)
            if k < 3:
                csend[k, i, 0] = real.astype(BF16)
                csend[k, i, 1] = imag.astype(BF16)
            else:
                cons[i, 0] = real
                cons[i, 1] = imag
        if k < 3:
            who = {"band": peer, "slab": s}
            copy = remote(csend.at[k], crecv.at[k], send_c.at[k], recv_c.at[k], who)
            copy.start()
            cons_copies.append(copy)

    sent_by_side(halo_copies, "wait_send")
    every(image_copies, "wait_send")

    arrived("noise")
    size = jnp.full((16, Y), step[0], F32)
    spread = jnp.sqrt(2.0 * size)
    for g in range(2):
        for r in range(2):
            cons[g, r] = img[g, r] + spread * noise[g, r] - size * cons[g, r]
    wait_arrivals(score_copies)
    every(cons_copies, "wait_recv")
    gap = jnp.zeros((2, Y), F32)
    for g in range(2):
        consistency = []
        for r in range(2):
            v = cons[g, r]
            for k in range(1, nb):
                v = v - size * crecv[k - 1, g, r].astype(F32)
            consistency.append(v)
        for t in range(4):
            z = g * 4 + t
            v = score[z + 1, 0:8, :]
            below = jnp.where(low_ok, rrecv[0].astype(F32)[2 * z : 2 * z + 2, :], 0.0)
            above = jnp.where(high_ok, rrecv[1].astype(F32)[2 * z : 2 * z + 2, :], 0.0)
            if z in (0, 7):
                zside = 0 if z == 0 else 1
                ok = b > 0 if z == 0 else b < nb - 1
                v = v + jnp.where(ok, zrecv[zside].astype(F32), 0.0)
                below = below + jnp.where(ok & low_ok, erecv[0, zside].astype(F32)[0:2, :], 0.0)
                above = above + jnp.where(ok & high_ok, erecv[1, zside].astype(F32)[0:2, :], 0.0)
            v = v + jnp.concatenate(
                [below[0:1], gap, above[0:1], below[1:2], gap, above[1:2]], axis=0
            )
            for r in range(2):
                out[g, t, r] = size[0:4] * v[4 * r : 4 * r + 4, :] + consistency[r][4 * t : 4 * t + 4, :]
    sent_by_side(score_copies, "wait_send")
    every(cons_copies, "wait_send")


def per_device(
    current_image,
    langevin_noise,
    step_size,
    coil_maps,
    measured_kspace,
    sample_mask,
    caipi_steps,
    band_order,
    weight_in,
    weight_mid,
    weight_out,
):
    w_in = jnp.transpose(weight_in, (2, 3, 4, 1, 0)).reshape(27, 2, CH)
    w_mid = jnp.transpose(weight_mid, (2, 3, 4, 0, 1)).reshape(27, CH, CH)
    w_out = jnp.transpose(weight_out, (2, 3, 4, 0, 1)).reshape(27, 2, CH)
    consts = [jnp.asarray(c) for c in constants()]
    dma = pltpu.SemaphoreType.DMA
    vmem = pltpu.VMEM
    tile = (16, Y)
    return pl.pallas_call(
        kernel,
        out_shape=jax.ShapeDtypeStruct(current_image.shape, F32),
        in_specs=[pl.BlockSpec(memory_space=pl.ANY)] * 16,
        out_specs=pl.BlockSpec(memory_space=pltpu.VMEM),
        scratch_shapes=[
            vmem((2, 2) + tile, F32),
            vmem((2, 2) + tile, F32),
            pltpu.SMEM((1,), F32),
            vmem((NB, 2) + tile, BF16),
            vmem((2, 2) + tile, BF16),
            vmem((2, 2) + tile, BF16),
            vmem((2, 2, 8, Y), BF16),
            vmem((2, 2, 8, Y), BF16),
            vmem((2, 2, 8, Y), BF16),
            vmem((2, 2, 8, Y), BF16),
            vmem((2,) + tile, BF16),
            vmem((2,) + tile, BF16),
            vmem((2, 8, Y), BF16),
            vmem((2, 8, Y), BF16),
            vmem((2, 2, 8, Y), BF16),
            vmem((2, 2, 8, Y), BF16),
            vmem((3, 2, 2) + tile, BF16),
            vmem((3, 2, 2) + tile, BF16),
            vmem((NB, NC, 2) + tile, BF16),
            vmem((NB, NC, 2) + tile, BF16),
            vmem((2, NC) + tile, F32),
            vmem((NS, Y), jnp.int32),
            pltpu.SMEM((NB,), jnp.int32),
            pltpu.SMEM((NB,), jnp.int32),
            vmem((27, 2, CH), BF16),
            vmem((27, CH, CH), BF16),
            vmem((27, 2, CH), BF16),
            vmem((3 * Y, Y), BF16),
            vmem((Y, 2 * Y), BF16),
            vmem((Y, 2 * Y), BF16),
            vmem((6, 144, 54), BF16),
            vmem((4, 144, 54), BF16),
            vmem((144, 6 * CH), BF16),
            vmem((256, 8 * 256), BF16),
            vmem((2, 256, 256), BF16),
            vmem((144, 4 * CH), BF16),
            vmem((NB, 2) + tile, F32),
            vmem((2, NC) + tile, F32),
            vmem((12 * 48, Y), BF16),
            vmem((10, Y + 32, 6 * CH), BF16),
            vmem((8, Y, 4 * CH), BF16),
            vmem((8, 144, Y), F32),
            vmem((10,) + tile, F32),
            vmem((2, 2) + tile, F32),
            dma((15, 8)),
            dma((3,)),
            dma((3,)),
            dma((2,)),
            dma((2,)),
            dma((4,)),
            dma((4,)),
            dma((2,)),
            dma((2,)),
            dma((2,)),
            dma((2,)),
            dma((2,)),
            dma((2,)),
            dma((4,)),
            dma((4,)),
            dma((3,)),
            dma((3,)),
        ],
        compiler_params=pltpu.CompilerParams(collective_id=0, has_side_effects=True, vmem_limit_bytes=40 * 1024 * 1024),
        name="langevin",
    )(
        *[
            v if v.shape == (1,) else pltpu.with_memory_space_constraint(v, pltpu.HBM)
            for v in (
                current_image, langevin_noise, step_size, coil_maps, measured_kspace, sample_mask,
                caipi_steps, band_order, w_in, w_mid, w_out, *consts,
            )
        ]
    )


def solution(mesh):
    in_specs = (
        P("band", None, None, "slab", None),
        P("band", None, None, "slab", None),
        P(),
        P(None, None, "band", None, "slab", None),
        P(None, "band", None, "slab", None),
        P(),
        P(),
        P(),
        P(),
        P(),
        P(),
    )
    out_specs = P("band", None, None, "slab", None)
    return jax.shard_map(
        per_device, mesh=mesh, in_specs=in_specs, out_specs=out_specs, check_vma=False
    )
```

```python
import functools
import math

import jax
import jax.numpy as jnp
import numpy as np
from jax import lax
from jax.experimental import pallas as pl
from jax.experimental.pallas import tpu as pltpu
from jax.sharding import PartitionSpec as P

MESH = pl.DeviceIdType.MESH
F32 = jnp.float32
BF16 = jnp.bfloat16
NB, NS, Y, NC, CH, ROWS = 8, 4, 384, 8, 64, 4
Q = Y // 16
LEAD = (2, 3, 4)


def column_of():
    p = np.arange(Y)
    return (p % 16) * Q + p // 16


def constants():
    col = column_of()
    perm = np.zeros((3, Y, Y), np.float32)
    for dx in range(3):
        for p in range(Y):
            c = col[p] + dx - 1
            if 0 <= c < Y:
                perm[dx, p, c] = 1.0
    k = np.arange(Y)
    phase = (np.outer(k, k) % Y).astype(np.float64) * (2.0 * math.pi / Y)
    table = np.concatenate([np.cos(phase), np.sin(phase)], axis=1) / math.sqrt(Y)
    table = table.astype(np.float32)
    high = table.astype(BF16)
    low = (table - high.astype(np.float32)).astype(BF16)
    row_at = [0, 1, 2, 3, -2, -1, 4, 5]
    place_in = np.zeros((6, 144, 54), np.float32)
    for ro in range(6):
        for dz in range(3):
            for dx in range(3):
                for ch in range(2):
                    for i, row in enumerate(row_at):
                        dy = row - (ro - 1) + 1
                        if 0 <= dy <= 2:
                            t = ((dz * 3 + dy) * 3 + dx) * 2 + ch
                            place_in[ro, dz * 48 + dx * 16 + ch * 8 + i, t] = 0.5
    place_out = np.zeros((4, 160, 54), np.float32)
    for rin in range(4):
        for dz in range(3):
            for dx in range(3):
                for ch in range(2):
                    for ro in range(-1, 5):
                        dy = rin - ro + 1
                        if 0 <= dy <= 2:
                            t = ((dz * 3 + dy) * 3 + dx) * 2 + ch
                            if ro == -1:
                                m = ch
                            elif ro == 4:
                                m = 2 + ch
                            else:
                                m = 80 + ch * 4 + ro
                            place_out[rin, (dz * 3 + dx) * 8 + m, t] = 1.0
    return (
        perm.reshape(3 * Y, Y).astype(BF16),
        high,
        low,
        place_in.astype(BF16),
        place_out.astype(BF16),
    )


def dot_nn(a, b):
    return jnp.dot(a, b, preferred_element_type=F32)


def dot_nt(a, b):
    return lax.dot_general(a, b, (((1,), (1,)), ((), ())), preferred_element_type=F32)


def dot_tn(a, b):
    return lax.dot_general(a, b, (((0,), (0,)), ((), ())), preferred_element_type=F32)


def kernel(
    image, noise_in, step_in, coil, measured, mask_in, steps_in, order_in, w_in, w_mid, w_out,
    perm_in, high_in, low_in, place1_in, place3_in,
    out,
    img, noise, step, imgbuf, hsend, hrecv, dsend, drecv, ssend, srecv,
    rsend, rrecv, zsend, zrecv, esend, erecv, csend, crecv,
    coilv, rolled, meas, maskv, steps, order, win, wmid, wout,
    perm, high, low, place1, place3,
    w1, w2, w2e, w3, rimg, data, xp, f1, f2, parts, score, cons,
    local, send_a, recv_a, send_h, recv_h, send_d, recv_d, send_s, recv_s,
    send_r, recv_r, send_z, recv_z, send_e, recv_e, send_c, recv_c,
):
    b = lax.axis_index("band")
    s = lax.axis_index("slab")
    nb = lax.axis_size("band")
    ns = lax.axis_size("slab")

    def at(db, ds_):
        return {"band": lax.rem(b + db + nb, nb), "slab": lax.rem(s + ds_ + ns, ns)}

    low_ok, high_ok = s > 0, s < ns - 1
    other = 1 - 2 * lax.rem(b, 2)
    across = lax.rem(b + 2, nb)
    peers = [across + other, across, b + other]
    groups = {}

    def fetch(name, index, pairs):
        copies = [pltpu.make_async_copy(src, dst, local.at[index, i]) for i, (src, dst) in enumerate(pairs)]
        for c in copies:
            c.start()
        groups[name] = copies

    def arrived(name):
        for c in groups.pop(name):
            c.wait()

    fetch("image", 0, [(image.at[g, t], img.at[g, :, pl.ds(4 * t, 4), :]) for g in range(2) for t in range(4)])
    barrier = pltpu.get_barrier_semaphore()

    def greet(ds_):
        for db in (0, -1, 1):
            pl.semaphore_signal(barrier, inc=1, device_id=at(db, ds_), device_id_type=MESH)

    pl.when(low_ok)(lambda: greet(-1))
    pl.when(high_ok)(lambda: greet(1))
    for peer in peers:
        pl.semaphore_signal(barrier, inc=1, device_id={"band": peer, "slab": s}, device_id_type=MESH)

    fetch("scalars", 1, [(steps_in, steps), (order_in, order), (step_in, step)])
    fetch("weights", 10, [(w_in, win), (w_mid, wmid), (w_out, wout), (place1_in, place1), (place3_in, place3)])
    fetch("perm", 11, [(perm_in, perm)])
    arrived("image")
    own = pl.multiple_of(2 * b, 2)
    for g in range(2):
        for r in range(2):
            imgbuf[own + g, r] = img[g, r].astype(BF16)
    for side in range(2):
        rows = [
            [img[g, r, 4 * t + 2 * side : 4 * t + 2 * side + 2, :] for g in range(2) for t in range(4)]
            for r in range(2)
        ]
        for r in range(2):
            hsend[side, r] = jnp.concatenate(rows[r], axis=0).astype(BF16)
        for zside in range(2):
            z0 = 0 if zside == 0 else 6
            dsend[side, zside] = jnp.concatenate(
                [rows[0][z0], rows[0][z0 + 1], rows[1][z0], rows[1][z0 + 1]], axis=0
            ).astype(BF16)
    for r in range(2):
        ssend[0, r] = img[0, r, 0:8, :].astype(BF16)
        ssend[1, r] = img[1, r, 8:16, :].astype(BF16)

    def remote(src, dst, ssem, rsem, who):
        return pltpu.make_async_remote_copy(
            src_ref=src, dst_ref=dst, send_sem=ssem, recv_sem=rsem, device_id=who, device_id_type=MESH
        )

    sides = (s + ns - 1) // ns + (2 * ns - 2 - s) // ns
    pl.semaphore_wait(barrier, len(peers) + 3 * sides)
    halo_copies = [[], [], []]
    for side in range(2):
        ds_ = -1 if side == 0 else 1
        halo_copies[side].append(
            remote(hsend.at[side], hrecv.at[1 - side], send_h.at[side], recv_h.at[1 - side], at(0, ds_))
        )
        for zside in range(2):
            db = -1 if zside == 0 else 1
            i, j = side * 2 + zside, (1 - side) * 2 + (1 - zside)
            halo_copies[side].append(
                remote(dsend.at[side, zside], drecv.at[1 - side, 1 - zside], send_d.at[i], recv_d.at[j], at(db, ds_))
            )
    for zside in range(2):
        db = -1 if zside == 0 else 1
        halo_copies[2].append(
            remote(ssend.at[zside], srecv.at[1 - zside], send_s.at[zside], recv_s.at[1 - zside], at(db, 0))
        )
    image_copies = [
        remote(
            imgbuf.at[pl.ds(own, 2)], imgbuf.at[pl.ds(own, 2)], send_a.at[k], recv_a.at[k],
            {"band": peer, "slab": s},
        )
        for k, peer in enumerate(peers)
    ]

    def every(copies, verb):
        for c in copies:
            getattr(c, verb)()

    def sent_by_side(copies, verb):
        pl.when(low_ok)(lambda: every(copies[0], verb))
        pl.when(high_ok)(lambda: every(copies[1], verb))
        every(copies[2], verb)

    def wait_arrivals(copies):
        pl.when(high_ok)(lambda: every(copies[0], "wait_recv"))
        pl.when(low_ok)(lambda: every(copies[1], "wait_recv"))
        every(copies[2], "wait_recv")

    sent_by_side(halo_copies, "start")
    every(image_copies, "start")

    for g in range(NB):
        fetch(
            f"coil{g}",
            2 + g,
            [
                (coil.at[g, t, :, r], coilv.at[g, :, r, pl.ds(4 * t, 4), :])
                for t in range(4)
                for r in range(2)
            ],
        )
    fetch("tables", 12, [(high_in, high), (low_in, low), (mask_in, maskv)])
    fetch(
        "meas",
        13,
        [(measured.at[t, :, r], meas.at[r, :, pl.ds(4 * t, 4), :]) for t in range(4) for r in range(2)],
    )
    fetch("noise", 14, [(noise_in.at[g, t], noise.at[g, :, pl.ds(4 * t, 4), :]) for g in range(2) for t in range(4)])

    arrived("weights")
    lane = lax.broadcasted_iota(jnp.int32, (1, 6 * CH), 1)
    inside = ((lane >= CH) | (s > 0)) & ((lane < 5 * CH) | (s < ns - 1))
    flat1 = jnp.concatenate([win[t].astype(F32) for t in range(27)], axis=0).astype(BF16)
    flat3 = jnp.concatenate([wout[t].astype(F32) for t in range(27)], axis=0).astype(BF16)
    w1v = jnp.concatenate([dot_nn(place1[r], flat1) for r in range(6)], axis=1)
    w1[...] = jnp.where(inside, w1v, 0.0).astype(BF16)
    w3[...] = jnp.concatenate([dot_nn(place3[r], flat3) for r in range(4)], axis=1).astype(BF16)
    none = jnp.zeros((CH, CH), F32)
    for dx in range(3):
        for dz in range(3):
            taps = [wmid[(dz * 3 + dy) * 3 + dx].astype(F32) * 0.5 for dy in range(3)]
            for ro in range(2):
                block = taps + [none] if ro == 0 else [none] + taps
                block = jnp.concatenate(block, axis=1).astype(BF16)
                for sl in range(2):
                    j = dz + sl
                    if j in (1, 2):
                        w2[pl.ds(sl * 128 + ro * CH, CH), pl.ds((dx * 2 + j - 1) * 256, 256)] = block
                    elif dx == 1:
                        w2[pl.ds(sl * 128 + ro * CH, CH), pl.ds((6 + sl) * 256, 256)] = block
                    else:
                        w2e[sl, pl.ds(dx // 2 * 128 + ro * CH, CH), :] = block
    w2[pl.ds(128, 128), pl.ds(6 * 256, 256)] = jnp.zeros((128, 256), BF16)
    w2[pl.ds(0, 128), pl.ds(7 * 256, 256)] = jnp.zeros((128, 256), BF16)

    arrived("scalars")
    shifts = [steps[order[g]] * (Y // 8) for g in range(NB)]
    for g in range(NB):
        arrived(f"coil{g}")
        for c in range(NC):
            for r in range(2):
                rolled[g, c, r] = pltpu.roll(coilv[g, c, r], shifts[g], 1)

    wait_arrivals(halo_copies)
    arrived("perm")
    tiles = []
    for i in range(12):
        z = i - 2
        pieces = []
        if z < 0:
            t = z + 2
            ok = b > 0
            halo = [drecv[side, 0] for side in range(2)]
            offset, stride = (z + 2) * 2, 4
        elif z > 7:
            t = z - 8
            ok = b < nb - 1
            halo = [drecv[side, 1] for side in range(2)]
            offset, stride = (z - 8) * 2, 4
        else:
            t = z % 4
            ok = None
            halo = None
        for r in range(2):
            if halo is None:
                mine = imgbuf[own + z // 4, r].astype(F32)[4 * t : 4 * t + 4, :]
                below = hrecv[0, r].astype(F32)[2 * z : 2 * z + 2, :]
                above = hrecv[1, r].astype(F32)[2 * z : 2 * z + 2, :]
            else:
                mine = srecv[0 if z < 0 else 1, r].astype(F32)[4 * t : 4 * t + 4, :]
                o = r * stride + offset
                below = halo[0].astype(F32)[o : o + 2, :]
                above = halo[1].astype(F32)[o : o + 2, :]
            below = jnp.where(low_ok, below, 0.0)
            above = jnp.where(high_ok, above, 0.0)
            pieces += [mine, below, above]
        tile = jnp.concatenate(pieces, axis=0)
        if ok is not None:
            tile = jnp.where(ok, tile, 0.0)
        tiles.append(tile.astype(BF16))
    field = jnp.concatenate(tiles, axis=0)
    for dx in range(3):
        moved = dot_nt(field, perm[pl.ds(dx * Y, Y), :]).astype(BF16)
        for i in range(12):
            xp[pl.ds(i * 48 + dx * 16, 16), :] = moved[16 * i : 16 * i + 16, :]

    sub = lax.broadcasted_iota(jnp.int32, (16, 6 * CH), 0)

    for z in range(10):
        x = xp[pl.ds(z * 48, 144), :]
        if z == 0:
            x = jnp.where(b > 0, x, jnp.zeros_like(x))
        if z == 9:
            x = jnp.where(b < nb - 1, x, jnp.zeros_like(x))
        h = dot_tn(x, w1[...])
        f = h + h * jnp.tanh(h)
        f1[z, pl.ds(16, Y), :] = f.astype(BF16)
        left = jnp.where(sub == 0, 0.0, pltpu.roll(f[Y - 16 :, :], 1, 0))
        right = jnp.where(sub == 15, 0.0, pltpu.roll(f[:16, :], 15, 0))
        f1[z, pl.ds(0, 16), :] = left.astype(BF16)
        f1[z, pl.ds(Y + 16, 16), :] = right.astype(BF16)

    every(image_copies, "wait_recv")
    for g in range(NB):
        for r in range(2):
            rimg[g, r] = pltpu.roll(imgbuf[g, r].astype(F32), shifts[g], 1)

    def collapse(c):
        real = jnp.zeros((16, Y), F32)
        imag = jnp.zeros((16, Y), F32)
        for g in range(NB):
            a_re = rolled[g, c, 0].astype(F32)
            a_im = rolled[g, c, 1].astype(F32)
            b_re = rimg[g, 0]
            b_im = rimg[g, 1]
            real += a_re * b_re - a_im * b_im
            imag += a_re * b_im + a_im * b_re
        data[0, c] = real
        data[1, c] = imag

    def middle(zp, carry):
        for rp in range(2):
            lanes = pl.ds(rp * 128, 256)
            views = [f1[2 * zp + j, pl.ds(16 * dx, Y), lanes] for dx in range(3) for j in (1, 2)]
            views += [f1[2 * zp + j, pl.ds(16, Y), lanes] for j in (0, 3)]
            h = dot_nt(jnp.concatenate(views, axis=1), w2[...])
            for sl in range(2):
                side = dot_nt(f1[2 * zp + 3 * sl, :, lanes], w2e[sl])
                v = h[:, sl * 128 : sl * 128 + 128] + side[:Y, :128] + side[32:, 128:]
                f2[2 * zp + sl, :, pl.ds(rp * 128, 128)] = (v + v * jnp.tanh(v)).astype(BF16)
        return carry

    lax.fori_loop(0, 4, middle, 0)

    def scores(half):
        for z in range(8):
            parts[half, z] = dot_nt(w3[pl.ds(80 * half, 80), :], f2[z])
        both = []
        for dx in range(3):
            sums = []
            for zo in range(10):
                terms = [
                    parts[half, zo + dz - 2, pl.ds((dz * 3 + dx) * 8, 8), :]
                    for dz in range(3)
                    if 0 <= zo + dz - 2 < 8
                ]
                sums.append(functools.reduce(jnp.add, terms))
            total = jnp.concatenate(sums, axis=0)
            top = total.astype(BF16)
            rest = (total - top.astype(F32)).astype(BF16)
            both.append(jnp.concatenate([top, rest], axis=0))
        both = dot_nn(jnp.concatenate(both[::-1], axis=1), perm[...])
        score[half] = (both[:80] + both[80:]).reshape(10, 8, Y)

    scores(0)
    for side in range(2):
        o = 2 * side
        rsend[side] = jnp.concatenate([score[0, z + 1, o : o + 2, :] for z in range(8)], axis=0).astype(BF16)
        zi = 0 if side == 0 else 9
        for rside in range(2):
            o = 2 * rside
            pad = jnp.zeros((6, Y), F32)
            esend[rside, side] = jnp.concatenate([score[0, zi, o : o + 2, :], pad], axis=0).astype(BF16)
    score_copies = [[], [], []]
    for side in range(2):
        d = -1 if side == 0 else 1
        score_copies[side].append(
            remote(rsend.at[side], rrecv.at[1 - side], send_r.at[side], recv_r.at[1 - side], at(0, d))
        )
        for zside in range(2):
            db = -1 if zside == 0 else 1
            i, j = side * 2 + zside, (1 - side) * 2 + (1 - zside)
            score_copies[side].append(
                remote(esend.at[side, zside], erecv.at[1 - side, 1 - zside], send_e.at[i], recv_e.at[j], at(db, d))
            )
    for side in range(2):
        d = -1 if side == 0 else 1
        score_copies[2].append(
            remote(zsend.at[side], zrecv.at[1 - side], send_z.at[side], recv_z.at[1 - side], at(d, 0))
        )
    pl.when(low_ok)(lambda: every(score_copies[0], "start"))
    pl.when(high_ok)(lambda: every(score_copies[1], "start"))

    def collapses(c, carry):
        collapse(c)
        return carry

    lax.fori_loop(0, NC, collapses, 0)
    arrived("tables")
    arrived("meas")

    def transform(field):
        flat = field.reshape(2 * NC * 16, Y)
        top = flat.astype(BF16)
        rest = (flat - top.astype(F32)).astype(BF16)
        lhs = jnp.concatenate([top, rest, top], axis=1)
        rhs = jnp.concatenate([high[...], high[...], low[...]], axis=0)
        both = dot_nn(lhs, rhs)
        half = NC * 16
        return both[:half, :Y], both[:half, Y:], both[half:, :Y], both[half:, Y:]

    re_c, re_s, im_c, im_s = transform(data[...])
    keep = maskv[...].astype(F32)
    keep = jnp.concatenate([jnp.broadcast_to(keep[t : t + 1], (4, Y)) for t in range(4)], axis=0)[None]
    data[0] = keep * ((re_c + im_s).reshape(NC, 16, Y) - meas[0])
    data[1] = keep * ((im_c - re_s).reshape(NC, 16, Y) - meas[1])
    re_c, re_s, im_c, im_s = transform(data[...])
    data[0] = (re_c - im_s).reshape(NC, 16, Y)
    data[1] = (im_c + re_s).reshape(NC, 16, Y)

    cons_copies = []
    for k, peer in enumerate(peers + [b]):
        for i in range(2):
            g = 2 * peer + i
            real = jnp.zeros((16, Y), F32)
            imag = jnp.zeros((16, Y), F32)
            for c in range(NC):
                a_re = rolled[g, c, 0].astype(F32)
                a_im = rolled[g, c, 1].astype(F32)
                real += a_re * data[0, c] + a_im * data[1, c]
                imag += a_re * data[1, c] - a_im * data[0, c]
            back = lax.rem(Y - steps[order[g]] * (Y // 8), Y)
            real = pltpu.roll(real, back, 1)
            imag = pltpu.roll(imag, back, 1)
            if k < 3:
                csend[k, i, 0] = real.astype(BF16)
                csend[k, i, 1] = imag.astype(BF16)
            else:
                cons[i, 0] = real
                cons[i, 1] = imag
        if k < 3:
            who = {"band": peer, "slab": s}
            copy = remote(csend.at[k], crecv.at[k], send_c.at[k], recv_c.at[k], who)
            copy.start()
            cons_copies.append(copy)

    scores(1)
    for side in range(2):
        zsend[side] = score[1, 9 * side].astype(BF16)
    every(score_copies[2], "start")
    sent_by_side(halo_copies, "wait_send")
    every(image_copies, "wait_send")

    arrived("noise")
    size = jnp.full((16, Y), step[0], F32)
    spread = jnp.sqrt(2.0 * size)
    for g in range(2):
        for r in range(2):
            cons[g, r] = img[g, r] + spread * noise[g, r] - size * cons[g, r]
    wait_arrivals(score_copies)
    every(cons_copies, "wait_recv")
    gap = jnp.zeros((2, Y), F32)
    for g in range(2):
        consistency = []
        for r in range(2):
            v = cons[g, r]
            for k in range(1, nb):
                v = v - size * crecv[k - 1, g, r].astype(F32)
            consistency.append(v)
        for t in range(4):
            z = g * 4 + t
            v = score[1, z + 1]
            below = jnp.where(low_ok, rrecv[0].astype(F32)[2 * z : 2 * z + 2, :], 0.0)
            above = jnp.where(high_ok, rrecv[1].astype(F32)[2 * z : 2 * z + 2, :], 0.0)
            if z in (0, 7):
                zside = 0 if z == 0 else 1
                ok = b > 0 if z == 0 else b < nb - 1
                v = v + jnp.where(ok, zrecv[zside].astype(F32), 0.0)
                below = below + jnp.where(ok & low_ok, erecv[0, zside].astype(F32)[0:2, :], 0.0)
                above = above + jnp.where(ok & high_ok, erecv[1, zside].astype(F32)[0:2, :], 0.0)
            v = v + jnp.concatenate(
                [below[0:1], gap, above[0:1], below[1:2], gap, above[1:2]], axis=0
            )
            for r in range(2):
                out[g, t, r] = size[0:4] * v[4 * r : 4 * r + 4, :] + consistency[r][4 * t : 4 * t + 4, :]
    sent_by_side(score_copies, "wait_send")
    every(cons_copies, "wait_send")


def per_device(
    current_image,
    langevin_noise,
    step_size,
    coil_maps,
    measured_kspace,
    sample_mask,
    caipi_steps,
    band_order,
    weight_in,
    weight_mid,
    weight_out,
):
    w_in = jnp.transpose(weight_in, (2, 3, 4, 1, 0)).reshape(27, 2, CH)
    w_mid = jnp.transpose(weight_mid, (2, 3, 4, 0, 1)).reshape(27, CH, CH)
    w_out = jnp.transpose(weight_out, (2, 3, 4, 0, 1)).reshape(27, 2, CH)
    consts = [jnp.asarray(c) for c in constants()]
    dma = pltpu.SemaphoreType.DMA
    vmem = pltpu.VMEM
    tile = (16, Y)
    return pl.pallas_call(
        kernel,
        out_shape=jax.ShapeDtypeStruct(current_image.shape, F32),
        in_specs=[pl.BlockSpec(memory_space=pl.ANY)] * 16,
        out_specs=pl.BlockSpec(memory_space=pltpu.VMEM),
        scratch_shapes=[
            vmem((2, 2) + tile, F32),
            vmem((2, 2) + tile, F32),
            pltpu.SMEM((1,), F32),
            vmem((NB, 2) + tile, BF16),
            vmem((2, 2) + tile, BF16),
            vmem((2, 2) + tile, BF16),
            vmem((2, 2, 8, Y), BF16),
            vmem((2, 2, 8, Y), BF16),
            vmem((2, 2, 8, Y), BF16),
            vmem((2, 2, 8, Y), BF16),
            vmem((2,) + tile, BF16),
            vmem((2,) + tile, BF16),
            vmem((2, 8, Y), BF16),
            vmem((2, 8, Y), BF16),
            vmem((2, 2, 8, Y), BF16),
            vmem((2, 2, 8, Y), BF16),
            vmem((3, 2, 2) + tile, BF16),
            vmem((3, 2, 2) + tile, BF16),
            vmem((NB, NC, 2) + tile, BF16),
            vmem((NB, NC, 2) + tile, BF16),
            vmem((2, NC) + tile, F32),
            vmem((NS, Y), jnp.int32),
            pltpu.SMEM((NB,), jnp.int32),
            pltpu.SMEM((NB,), jnp.int32),
            vmem((27, 2, CH), BF16),
            vmem((27, CH, CH), BF16),
            vmem((27, 2, CH), BF16),
            vmem((3 * Y, Y), BF16),
            vmem((Y, 2 * Y), BF16),
            vmem((Y, 2 * Y), BF16),
            vmem((6, 144, 54), BF16),
            vmem((4, 160, 54), BF16),
            vmem((144, 6 * CH), BF16),
            vmem((256, 8 * 256), BF16),
            vmem((2, 256, 256), BF16),
            vmem((160, 4 * CH), BF16),
            vmem((NB, 2) + tile, F32),
            vmem((2, NC) + tile, F32),
            vmem((12 * 48, Y), BF16),
            vmem((10, Y + 32, 6 * CH), BF16),
            vmem((8, Y, 4 * CH), BF16),
            vmem((2, 8, 80, Y), F32),
            vmem((2, 10, 8, Y), F32),
            vmem((2, 2) + tile, F32),
            dma((15, 8)),
            dma((3,)),
            dma((3,)),
            dma((2,)),
            dma((2,)),
            dma((4,)),
            dma((4,)),
            dma((2,)),
            dma((2,)),
            dma((2,)),
            dma((2,)),
            dma((2,)),
            dma((2,)),
            dma((4,)),
            dma((4,)),
            dma((3,)),
            dma((3,)),
        ],
        compiler_params=pltpu.CompilerParams(collective_id=0, has_side_effects=True, vmem_limit_bytes=40 * 1024 * 1024),
        name="langevin",
    )(
        *[
            v if v.shape == (1,) else pltpu.with_memory_space_constraint(v, pltpu.HBM)
            for v in (
                current_image, langevin_noise, step_size, coil_maps, measured_kspace, sample_mask,
                caipi_steps, band_order, w_in, w_mid, w_out, *consts,
            )
        ]
    )


def solution(mesh):
    in_specs = (
        P("band", None, None, "slab", None),
        P("band", None, None, "slab", None),
        P(),
        P(None, None, "band", None, "slab", None),
        P(None, "band", None, "slab", None),
        P(),
        P(),
        P(),
        P(),
        P(),
        P(),
    )
    out_specs = P("band", None, None, "slab", None)
    return jax.shard_map(
        per_device, mesh=mesh, in_specs=in_specs, out_specs=out_specs, check_vma=False
    )
```
